256 devices in a mesh: ep: 64 (over z, x, core), tp: 4 (over y).
Axes of the slice: x: 4, y: 4, z: 8, core: 2. Of those that a mesh axis runs over, the one named last changes fastest.
Arguments:
- tokens: bfloat16 [2, 1024, 4096], P(None, 'ep'), may hold values from -6 to 6
- route_ids: int32 [2, 1024, 8], P(None, 'ep'), may hold values from 0 to 15, all different within a row; in each aligned block of 16 rows (0 to 15, 16 to 31, ..., all dimensions but the last counted through in order) at most 10 rows name the same one
- route_weights: float32 [2, 1024, 8], P(None, 'ep'), may hold values from 0.1 to 0.4
- train_map: int32 [64], replicated, may hold values from 0 to 63, each once
- serve_place: int32 [64], replicated, may hold values from 0 to 15, as said below
- train_gate: bfloat16 [64, 1024, 1536], P('ep', None, 'tp'), may hold values from -0.09375 to 0.09375
- train_up: bfloat16 [64, 1024, 1536], P('ep', None, 'tp'), may hold values from -0.09375 to 0.09375
- train_down: bfloat16 [64, 1024, 1536], P('ep', None, 'tp'), may hold values from -0.15625 to 0.15625
Outputs:
- serve_gate: bfloat16 [64, 4096, 1536], P('ep', None, 'tp')
- serve_up: bfloat16 [64, 4096, 1536], P('ep', None, 'tp')
- serve_down: bfloat16 [64, 4096, 1536], P('ep', None, 'tp')
- moe_out: bfloat16 [2, 1024, 4096], P(None, 'ep', 'tp')
The draws below stay inside these ranges and needn't reach their ends.
Inputs may be any that keep to these rules, and one draw needn't show every extreme that they name: `route_ids`: each row names 8 different experts; in each aligned block of 16 rows (one index of ep in one step) no expert is named by more than 10 rows. `train_map`: each trainer slot holds a different piece; piece q is part q % 4 of expert q // 4. `serve_place`: every expert occupies two or more serving slots, and some expert exactly two.
All inputs are finite; a program needn't handle non-finite values.
Results may differ from the reference program's by a relative error of at most 0.012.
Values may be sent and summed in bfloat16 or wider, within the bound.
No kernel may reach another device: no remote copies, remote signals or barrier semaphores. Data moves between devices by JAX's collectives and lax.ppermute only.
A program may use at most 128 MiB of HBM per device.

```python
import math
import jax
import jax.numpy as jnp
import numpy as np
from jax import lax

D = 4096
FF = 1536
TOPK = 8
EXPERTS = 16
SLOTS = 64
STEPS = 2
TOK_DEV = 16
PARTS_SIZE = 4
QUARTER = 384
TOKENS = 1024
MOST = 10
N_EP = 64


def draw_serve_place(key, part):
    key_spare = jax.random.fold_in(key, 101)
    key_first = jax.random.fold_in(key, 202)
    key_second = jax.random.fold_in(key, 303)
    key_shuffle = jax.random.fold_in(key, 404)
    initial = jnp.arange(2 * EXPERTS, dtype=jnp.int32) % EXPERTS
    spare_expert = jax.random.randint(key_spare, (), 0, EXPERTS, dtype=jnp.int32)
    extra_slots = SLOTS - 2 * EXPERTS
    first_factor = jax.random.randint(key_first, (extra_slots,), 0, EXPERTS - 1, dtype=jnp.int32)
    second_factor = jax.random.randint(key_second, (extra_slots,), 0, EXPERTS - 1, dtype=jnp.int32)
    offset = first_factor * second_factor // (EXPERTS - 1)
    extra_experts = (spare_expert + 1 + offset) % EXPERTS
    combined = jnp.concatenate([initial, extra_experts.astype(jnp.int32)])
    shuffle = jax.random.permutation(key_shuffle, SLOTS)
    return combined[shuffle].astype(jnp.int32)


def levels(stream_key, shape, cuts, smallest, high):
    def one(position, shards_of):
        heights = jax.random.uniform(jax.random.fold_in(jax.random.fold_in(stream_key, 6), position), (shards_of,), jnp.float32, smallest / len(cuts), high / len(cuts))
        return jnp.repeat(jnp.exp(heights), shape[position] // shards_of).reshape((-1,) + (1,) * (len(shape) - position - 1))

    loudness = one(*cuts[0])
    for cut in cuts[1:]:
        loudness = loudness * one(*cut)
    return loudness


def assign_block(rng, own, number, rows, count, top, reach, slope):
    ranking = jax.random.permutation(rng, count)
    crowded, common = shares(count, rows * top, reach, slope, True), shares(count, rows * top, reach, slope, False)
    places = jnp.arange(count)

    def named(tallies, rotation):
        used = int((tallies > 0).sum())
        fixed = max(1, used // 4)
        moved = fixed + (places - fixed + rotation * (used - fixed)) % max(1, count - fixed)
        return jnp.zeros((count,), jnp.int32).at[ranking[jnp.where(places < fixed, places, moved)]].set(jnp.asarray(tallies, jnp.int32))

    tallies = jnp.where(number % 4 == 0, named(crowded, number // 4), named(common, number - number // 4 - 1))
    mixed = jax.random.permutation(jax.random.fold_in(own, 3), count)
    donor, taker = mixed[0:count // 2 * 2:2], mixed[1:count // 2 * 2:2]
    slack = jnp.minimum(tallies[donor] - 1, reach - tallies[taker]) // 2
    slack = jnp.where((donor == ranking[0]) | (taker == ranking[0]) | (tallies[taker] == 0), 0, jnp.maximum(slack, 0))
    moved = jax.random.randint(jax.random.fold_in(own, 4), (count // 2,), 0, 1 << 20) % (slack + 1)
    tallies = tallies.at[donor].add(-moved).at[taker].add(moved)
    members = jnp.searchsorted(jnp.cumsum(tallies), jnp.arange(rows * top), side="right").astype(jnp.int32)
    grid = members.reshape(top, rows).T
    grid = grid[jax.random.permutation(jax.random.fold_in(own, 1), rows)]
    rotation = jax.random.randint(jax.random.fold_in(own, 2), (rows, 1), 0, top)
    return jnp.take_along_axis(grid, (jnp.arange(top)[None, :] + rotation) % top, axis=1)


def shares(count, total, bound, lean, full):
    weights = [(1 << 20) // math.isqrt(grade ** lean) + 1 for grade in range(1, count + 1)]
    largest = bound if full else min(bound, max(-(-total // count), total * weights[0] // sum(weights)))
    least = 1 if total - largest >= count - 1 else 0
    given, spare = [largest] + [least] * (count - 1), total - largest - least * (count - 1)
    while spare > 0:
        movable = [i for i in range(1, count) if given[i] < largest] or [i for i in range(1, count) if given[i] < bound]
        pool, budget = sum([weights[i] for i in movable]), spare
        for i in movable:
            more = min(bound - given[i], max(1, budget * weights[i] // pool), spare)
            given[i] = given[i] + more
            spare = spare - more
    return np.array(given)


def scatter_about(own_key, shape, spread, limit, cuts=(), kind=jnp.bfloat16):
    factor_of = levels(own_key, shape, cuts, -0.22, 0.18) if cuts else 1.0
    result = jax.random.normal(own_key, shape, jnp.float32) * spread * factor_of
    return jnp.minimum(jnp.maximum(result, -limit), limit).astype(kind)


def setup_inputs(seed: int = 0) -> dict:
    key_list = jax.random.split(jax.random.key(seed), 9)
    tokens = scatter_about(key_list[0], (STEPS, TOKENS, D), 1.0, 6.0, ((1, 64),))
    route_ids_keys = jax.random.split(jax.random.fold_in(key_list[1], 1), STEPS * TOKENS // TOK_DEV)
    route_ids_turns = jax.random.permutation(jax.random.fold_in(key_list[1], 3), STEPS * TOKENS // TOK_DEV)
    route_ids = jax.vmap(lambda own, number: assign_block(jax.random.fold_in(key_list[1], 2), own, number, TOK_DEV, EXPERTS, TOPK, MOST, 2))(route_ids_keys, route_ids_turns).reshape((STEPS, TOKENS, TOPK))
    route_weights = jnp.clip(0.1 + 0.3 * jax.random.uniform(key_list[2], (STEPS, TOKENS, TOPK), jnp.float32) ** levels(key_list[2], (STEPS, TOKENS, TOPK), ((1, 64),), -0.2, 0.2), 0.1, 0.4)
    train_map = jax.random.permutation(key_list[3], SLOTS).astype(jnp.int32)
    serve_place = draw_serve_place(jax.random.fold_in(key_list[8], 71), 0)
    train_gate = scatter_about(key_list[5], (SLOTS, D // PARTS_SIZE, FF), D ** -0.5, 0.09375, ((0, 64), (2, 4)))
    train_up = scatter_about(key_list[6], (SLOTS, D // PARTS_SIZE, FF), D ** -0.5, 0.09375, ((0, 64), (2, 4)))
    train_down = scatter_about(key_list[7], (SLOTS, D // PARTS_SIZE, FF), FF ** -0.5, 0.15625, ((0, 64), (2, 4)))
    return {"tokens": tokens, "route_ids": route_ids, "route_weights": route_weights, "train_map": train_map, "serve_place": serve_place, "train_gate": train_gate, "train_up": train_up, "train_down": train_down}


def reference(tokens, route_ids, route_weights, train_map, serve_place, train_gate, train_up, train_down):
    inverse = jnp.argsort(train_map).astype(jnp.int32)
    expert_gate = train_gate[inverse].reshape(EXPERTS, D, FF)
    expert_up = train_up[inverse].reshape(EXPERTS, D, FF)
    expert_down = train_down[inverse].reshape(EXPERTS, D, FF)
    place_index = serve_place.astype(jnp.int32)
    serve_gate = expert_gate[place_index]
    serve_up = expert_up[place_index]
    serve_down = expert_down[place_index]
    capacity = min(TOKENS, N_EP * MOST)
    results = []
    for decode_step in range(STEPS):
        pair_experts = route_ids[decode_step].reshape(-1)
        pair_weights = route_weights[decode_step].reshape(-1)
        step_tokens = tokens[decode_step]

        def add_expert(expert, running):
            matches = pair_experts == expert
            ordering = jnp.argsort(jnp.where(matches, 0, 1).astype(jnp.int32), stable=True)[:capacity].astype(jnp.int32)
            valid_pair = matches[ordering]
            token_rows = (ordering // TOPK).astype(jnp.int32)
            inputs = step_tokens[token_rows]
            gate_act = jnp.dot(inputs, expert_gate[expert], preferred_element_type=jnp.float32)
            up_act = jnp.dot(inputs, expert_up[expert], preferred_element_type=jnp.float32)
            hidden = (jax.nn.silu(gate_act) * up_act).astype(jnp.bfloat16)
            down_rows = expert_down[expert]
            summed = jnp.zeros((capacity, D), jnp.float32)
            for quarter_index in range(FF // QUARTER):
                lower = quarter_index * QUARTER
                partial_value = jnp.dot(hidden[:, lower:lower + QUARTER], down_rows[:, lower:lower + QUARTER].T, preferred_element_type=jnp.float32).astype(jnp.bfloat16)
                partial_value = lax.optimization_barrier(partial_value)
                summed = summed + partial_value.astype(jnp.float32)
            expert_out = summed.astype(jnp.bfloat16)
            pair_scale = jnp.where(valid_pair, pair_weights[ordering], jnp.zeros_like(pair_weights[ordering]))
            return running.at[token_rows].add(pair_scale[:, None] * expert_out.astype(jnp.float32))

        running = lax.fori_loop(0, EXPERTS, add_expert, jnp.zeros((TOKENS, D), jnp.float32))
        results.append(running.astype(jnp.bfloat16))
    return serve_gate, serve_up, serve_down, jnp.stack(results)
```

```python
import jax
import jax.numpy as jnp
from jax import lax
from jax.sharding import Mesh, PartitionSpec as P

EXPERTS = 16
MOST = 10
Z, X, C, Y = 8, 4, 2, 4
PLANE = X * C
EP = ("z", "x", "c")
XC = ("x", "c")
DOWN_CHUNKS = 2


def exchange(value, axes):
    return lax.all_to_all(value, axes, split_axis=0, concat_axis=0, tiled=True)


def shift(value, step):
    return lax.ppermute(value, "z", [(i, (i + step) % Z) for i in range(Z)])


def gather_planes(block):
    ahead = [block]
    behind = [block]
    for _ in range(Z // 2 - 1):
        behind.append(shift(behind[-1], 1))
        ahead.append(shift(ahead[-1], -1))
    half = block.shape[0] // 2
    far = [shift(behind[-1][:half], 1), shift(ahead[-1][half:], -1)]
    return jnp.concatenate(ahead + far + behind[:0:-1], axis=0)


def take_rows(value, index):
    return value.at[index].get(mode="promise_in_bounds")


def body(
    tokens, route_ids, route_weights, train_map, serve_place, train_gate, train_up, train_down
):
    plane = lax.axis_index("z")
    line = lax.axis_index(XC)
    quarter = lax.axis_index("y")
    slot_count = serve_place.shape[0]
    part_count = slot_count // EXPERTS
    piece_rows = train_gate.shape[1]
    width = train_gate.shape[2]
    block_rows = piece_rows // PLANE
    steps, tok_count, model_width = tokens.shape
    out_width = model_width // Y
    own_tokens = steps * tok_count
    line_tokens = own_tokens * Z
    capacity = Z * steps * MOST // 2

    slot_iota = jnp.arange(slot_count, dtype=jnp.int32)
    inverse = jnp.sum(
        jnp.where(train_map[:, None] == slot_iota[None, :], slot_iota[:, None], 0), axis=0
    )
    relative = (inverse - plane * PLANE + slot_count) % slot_count
    place_rank = jnp.sum(
        (serve_place[:, None] == serve_place[None, :])
        & (slot_iota[None, :] < slot_iota[:, None]),
        axis=1,
    )
    near_experts = lax.dynamic_slice(serve_place, (plane * PLANE,), (PLANE,))
    near_rank = lax.dynamic_slice(place_rank, (plane * PLANE,), (PLANE,))
    near_count = jnp.sum(near_experts[:, None] == serve_place[None, :], axis=1)
    wanted = near_experts[:, None] * part_count + jnp.arange(part_count, dtype=jnp.int32)[None, :]
    chosen = take_rows(relative, wanted)

    def spread(piece):
        return exchange(piece.reshape(PLANE, block_rows, width), XC)

    def relay(block):
        everything = gather_planes(block)
        return exchange(take_rows(everything, chosen), XC)

    def assemble(arrived):
        return jnp.swapaxes(arrived, 0, 1).reshape(1, part_count * piece_rows, width)

    block_gate = spread(train_gate)
    block_up = spread(train_up)
    block_down = spread(train_down).reshape(
        PLANE, DOWN_CHUNKS, block_rows // DOWN_CHUNKS, width
    )

    hot = route_ids.reshape(own_tokens, -1)[:, :, None] == jnp.arange(EXPERTS, dtype=jnp.int32)
    named = jnp.any(hot, axis=1).astype(jnp.float32)
    weight = jnp.sum(
        jnp.where(hot, route_weights.reshape(own_tokens, -1)[:, :, None], 0.0), axis=1
    )
    routes = lax.all_gather(jnp.concatenate([named, weight], axis=1), "z", axis=0, tiled=True)
    line_named = routes[:, :EXPERTS]
    line_weight = routes[:, EXPERTS:]
    own_rows = lax.dynamic_slice(
        tokens.reshape(own_tokens, model_width),
        (0, quarter * out_width),
        (own_tokens, out_width),
    )
    line_rows = lax.all_gather(own_rows, "z", axis=0, tiled=True)
    token_iota = jnp.arange(line_tokens, dtype=jnp.int32)
    earlier = (token_iota[None, :] < token_iota[:, None]).astype(jnp.bfloat16)
    seen = jnp.dot(
        earlier, line_named.astype(jnp.bfloat16), preferred_element_type=jnp.float32
    )
    near_hot = (near_experts[:, None] == jnp.arange(EXPERTS, dtype=jnp.int32)[None, :])

    def of_near(table):
        return jnp.sum(jnp.where(near_hot[:, None, :], table[None, :, :], 0.0), axis=2)

    near_named = of_near(line_named) > 0.5
    near_seen = of_near(seen).astype(jnp.int32)
    near_weight = of_near(line_weight)
    turn = (near_seen + line) % near_count[:, None]
    position = near_seen // near_count[:, None]
    sent = near_named & (turn == near_rank[:, None])
    placing = sent[:, None, :] & (
        position[:, None, :] == jnp.arange(capacity, dtype=jnp.int32)[None, :, None]
    )
    placing = placing.reshape(PLANE * capacity, line_tokens)
    send_rows = jnp.dot(
        placing.astype(jnp.bfloat16), line_rows, preferred_element_type=jnp.float32
    ).astype(jnp.bfloat16)
    received = exchange(send_rows, XC)
    inputs = lax.all_gather(received, "y", axis=0, tiled=False)

    mixing = jnp.where(
        placing.reshape(PLANE, capacity, line_tokens), near_weight[:, None, :], 0.0
    ).reshape(PLANE * capacity, line_tokens)
    mixing_high = mixing.astype(jnp.bfloat16)
    mixing_low = (mixing - mixing_high.astype(jnp.float32)).astype(jnp.bfloat16)

    serve_gate = assemble(relay(block_gate))
    serve_up = assemble(relay(block_up))
    by_part = (part_count, piece_rows, width)
    gate_act = jnp.einsum(
        "ymd,ydf->mf", inputs, serve_gate.reshape(by_part), preferred_element_type=jnp.float32
    )
    up_act = jnp.einsum(
        "ymd,ydf->mf", inputs, serve_up.reshape(by_part), preferred_element_type=jnp.float32
    )
    hidden = (jax.nn.silu(gate_act) * up_act).astype(jnp.bfloat16)

    arrived_down = []
    mixed = []
    for chunk in range(DOWN_CHUNKS):
        arrived = relay(block_down[:, chunk])
        arrived_down.append(arrived)
        partial_value = jnp.einsum(
            "mf,jyrf->ymjr", hidden, arrived, preferred_element_type=jnp.float32
        ).astype(jnp.bfloat16)
        rows = partial_value.shape[1]
        partial_value = partial_value.reshape(Y, rows, -1)
        expert_out = lax.psum_scatter(partial_value, "y", scatter_dimension=0, tiled=False)
        returned = exchange(expert_out, XC)
        line_out = sum(
            lax.dot_general(
                mixer, returned, (((0,), (0,)), ((), ())), preferred_element_type=jnp.float32
            )
            for mixer in (mixing_high, mixing_low)
        ).astype(jnp.bfloat16)
        home = exchange(line_out.reshape(Z, own_tokens, -1), "z")
        total = jnp.sum(home.astype(jnp.float32), axis=0).astype(jnp.bfloat16)
        mixed.append(total.reshape(steps, tok_count, PLANE, -1))
    serve_down = assemble(jnp.concatenate(arrived_down, axis=2))
    moe_out = jnp.concatenate(mixed, axis=3).reshape(steps, tok_count, out_width)
    return (serve_gate, serve_up, serve_down, moe_out)


def solution(mesh):
    fine = Mesh(mesh.devices.reshape(Z, X, C, Y), ("z", "x", "c", "y"))
    in_specs = (
        P(None, EP, None),
        P(None, EP, None),
        P(None, EP, None),
        P(),
        P(),
        P(EP, None, "y"),
        P(EP, None, "y"),
        P(EP, None, "y"),
    )
    out_specs = (P(EP, None, "y"), P(EP, None, "y"), P(EP, None, "y"), P(None, EP, "y"))
    return jax.shard_map(body, mesh=fine, in_specs=in_specs, out_specs=out_specs, check_vma=False)
```

```python
import jax
import jax.numpy as jnp
from jax import lax
from jax.sharding import Mesh, PartitionSpec as P

EXPERTS = 16
MOST = 10
Z, X, C, Y = 8, 4, 2, 4
PLANE = X * C
EP = ("z", "x", "c")
XC = ("x", "c")


def exchange(value, axes):
    return lax.all_to_all(value, axes, split_axis=0, concat_axis=0, tiled=True)


def shift(value, step):
    return lax.ppermute(value, "z", [(i, (i + step) % Z) for i in range(Z)])


def gather_planes(block):
    ahead = [block]
    behind = [block]
    for _ in range(Z // 2 - 1):
        behind.append(shift(behind[-1], 1))
        ahead.append(shift(ahead[-1], -1))
    half = block.shape[0] // 2
    far = [shift(behind[-1][:half], 1), shift(ahead[-1][half:], -1)]
    return jnp.concatenate(ahead + far + behind[:0:-1], axis=0)


def take_rows(value, index):
    return value.at[index].get(mode="promise_in_bounds")


def body(
    tokens, route_ids, route_weights, train_map, serve_place, train_gate, train_up, train_down
):
    plane = lax.axis_index("z")
    line = lax.axis_index(XC)
    quarter = lax.axis_index("y")
    slot_count = serve_place.shape[0]
    part_count = slot_count // EXPERTS
    piece_rows = train_gate.shape[1]
    width = train_gate.shape[2]
    block_rows = piece_rows // PLANE
    steps, tok_count, model_width = tokens.shape
    out_width = model_width // Y
    own_tokens = steps * tok_count
    line_tokens = own_tokens * Z
    capacity = Z * steps * MOST // 2

    slot_iota = jnp.arange(slot_count, dtype=jnp.int32)
    inverse = jnp.sum(
        jnp.where(train_map[:, None] == slot_iota[None, :], slot_iota[:, None], 0), axis=0
    )
    relative = (inverse - plane * PLANE + slot_count) % slot_count
    place_rank = jnp.sum(
        (serve_place[:, None] == serve_place[None, :])
        & (slot_iota[None, :] < slot_iota[:, None]),
        axis=1,
    )
    near_experts = lax.dynamic_slice(serve_place, (plane * PLANE,), (PLANE,))
    near_rank = lax.dynamic_slice(place_rank, (plane * PLANE,), (PLANE,))
    near_count = jnp.sum(near_experts[:, None] == serve_place[None, :], axis=1)
    wanted = near_experts[:, None] * part_count + jnp.arange(part_count, dtype=jnp.int32)[None, :]
    chosen = take_rows(relative, wanted)

    def spread(piece):
        return exchange(piece.reshape(PLANE, block_rows, width), XC)

    def relay(block):
        return take_rows(gather_planes(block), chosen)

    def assemble(arrived):
        return jnp.swapaxes(arrived, 0, 1).reshape(1, part_count * piece_rows, width)

    block_gate = spread(train_gate)
    block_up = spread(train_up)
    block_down = spread(train_down)

    experts = jnp.arange(EXPERTS, dtype=jnp.int32)
    hot = route_ids.reshape(own_tokens, -1)[:, :, None] == experts
    named = jnp.any(hot, axis=1).astype(jnp.bfloat16)
    weight = jnp.sum(
        jnp.where(hot, route_weights.reshape(own_tokens, -1)[:, :, None], 0.0), axis=1
    )
    high = weight.astype(jnp.bfloat16)
    rest = weight - high.astype(jnp.float32)
    middle = rest.astype(jnp.bfloat16)
    low = (rest - middle.astype(jnp.float32)).astype(jnp.bfloat16)
    own_rows = lax.dynamic_slice(
        tokens.reshape(own_tokens, model_width),
        (0, quarter * out_width),
        (own_tokens, out_width),
    )
    own_block = jnp.concatenate([own_rows, named, high, middle, low], axis=1)
    line_block = exchange(jnp.broadcast_to(own_block, (Z,) + own_block.shape), "z")
    line_block = line_block.reshape(line_tokens, -1)
    line_rows = line_block[:, :out_width]
    line_routes = line_block[:, out_width:]
    token_iota = jnp.arange(line_tokens, dtype=jnp.int32)
    earlier = (token_iota[None, :] < token_iota[:, None]).astype(jnp.bfloat16)
    near_hot = near_experts[:, None] == experts[None, :]

    def place(routes, line_index):
        names = routes[..., :EXPERTS]
        seen = jnp.einsum("ut,lte->lue", earlier, names, preferred_element_type=jnp.float32)

        def of_near(table):
            return jnp.sum(
                jnp.where(near_hot[None, :, None, :], table.astype(jnp.float32)[:, None], 0.0), axis=3
            )

        near_seen = of_near(seen).astype(jnp.int32)
        turn = (near_seen + line_index[:, None, None]) % near_count[None, :, None]
        position = near_seen // near_count[None, :, None]
        sent = (of_near(names) > 0.5) & (turn == near_rank[None, :, None])
        rows = jnp.arange(capacity, dtype=jnp.int32)[None, None, :, None]
        return sent[:, :, None, :] & (position[:, :, None, :] == rows)

    own_placing = place(line_routes[None], line[None])[0].astype(jnp.bfloat16)
    send_rows = jnp.einsum(
        "spt,td->spd", own_placing, line_rows, preferred_element_type=jnp.float32
    ).astype(jnp.bfloat16)
    route_rows = line_routes.reshape(-1, out_width)
    send_rows = jnp.concatenate(
        [send_rows, jnp.broadcast_to(route_rows, (PLANE,) + route_rows.shape)], axis=1
    )
    received = exchange(send_rows, XC)
    inputs = lax.all_gather(
        received[:, :capacity].reshape(PLANE * capacity, out_width), "y", axis=0, tiled=False
    )
    routes = received[:, capacity:].reshape(PLANE, line_tokens, -1)
    placing = place(routes, jnp.arange(PLANE, dtype=jnp.int32))
    weights = sum(
        routes[..., k * EXPERTS : (k + 1) * EXPERTS].astype(jnp.float32) for k in (1, 2, 3)
    )
    own_expert = lax.dynamic_slice(near_experts, (line,), (1,))
    own_weight = jnp.sum(jnp.where(experts == own_expert, weights, 0.0), axis=2)
    own_sent = lax.dynamic_slice(
        placing, (0, line, 0, 0), (PLANE, 1, capacity, line_tokens)
    )[:, 0]
    row_weight = jnp.sum(jnp.where(own_sent, own_weight[:, None, :], 0.0), axis=2)
    placing = placing.astype(jnp.bfloat16)

    serve_gate = assemble(exchange(relay(block_gate), XC))
    serve_up = assemble(exchange(relay(block_up), XC))
    by_part = (part_count, piece_rows, width)
    gate_act = jnp.einsum(
        "ymd,ydf->mf", inputs, serve_gate.reshape(by_part), preferred_element_type=jnp.float32
    )
    up_act = jnp.einsum(
        "ymd,ydf->mf", inputs, serve_up.reshape(by_part), preferred_element_type=jnp.float32
    )
    hidden = (jax.nn.silu(gate_act) * up_act * row_weight.reshape(-1, 1)).astype(jnp.bfloat16)

    plane_hidden = lax.all_gather(hidden, XC, axis=0, tiled=False).reshape(
        PLANE, PLANE, capacity, width
    )
    down_rows = relay(block_down)
    serve_down = assemble(exchange(down_rows, XC))
    partial_value = jnp.einsum(
        "slpf,syrf->slpyr", plane_hidden, down_rows, preferred_element_type=jnp.float32
    ).astype(jnp.bfloat16)
    plane_out = jnp.einsum(
        "lspt,slpyr->yltr", placing, partial_value, preferred_element_type=jnp.float32
    ).astype(jnp.bfloat16)
    line_out = lax.psum_scatter(
        plane_out.reshape(-1, block_rows), "y", scatter_dimension=0, tiled=True
    )
    home = exchange(
        jnp.swapaxes(line_out.reshape(PLANE, Z, own_tokens, block_rows), 0, 1).reshape(
            Z * PLANE, own_tokens, block_rows
        ),
        EP,
    )
    total = jnp.sum(
        home.reshape(Z, PLANE, own_tokens, block_rows).astype(jnp.float32), axis=0
    ).astype(jnp.bfloat16)
    moe_out = jnp.swapaxes(total, 0, 1).reshape(steps, tok_count, out_width)
    return (serve_gate, serve_up, serve_down, moe_out)


def solution(mesh):
    fine = Mesh(mesh.devices.reshape(Z, X, C, Y), ("z", "x", "c", "y"))
    in_specs = (
        P(None, EP, None),
        P(None, EP, None),
        P(None, EP, None),
        P(),
        P(),
        P(EP, None, "y"),
        P(EP, None, "y"),
        P(EP, None, "y"),
    )
    out_specs = (P(EP, None, "y"), P(EP, None, "y"), P(EP, None, "y"), P(None, EP, "y"))
    return jax.shard_map(body, mesh=fine, in_specs=in_specs, out_specs=out_specs, check_vma=False)
```

```python
import jax
import jax.numpy as jnp
from jax import lax
from jax.sharding import Mesh, PartitionSpec as P

EXPERTS = 16
MOST = 10
Z, X, C, Y = 8, 4, 2, 4
PLANE = X * C
EP = ("z", "x", "c")
XC = ("x", "c")


def exchange(value, axes):
    return lax.all_to_all(value, axes, split_axis=0, concat_axis=0, tiled=True)


def shift(value, step):
    return lax.ppermute(value, "z", [(i, (i + step) % Z) for i in range(Z)])


class Ring:
    def __init__(self, block):
        self.ahead = [block]
        self.behind = [block]
        self.far = []

    def hop(self):
        if len(self.ahead) < Z // 2:
            self.behind.append(shift(self.behind[-1], 1))
            self.ahead.append(shift(self.ahead[-1], -1))
        else:
            half = self.ahead[0].shape[0] // 2
            self.far = [shift(self.behind[-1][:half], 1), shift(self.ahead[-1][half:], -1)]
        return self

    def hold(self, value):
        last = self.far or [self.behind[-1], self.ahead[-1]]
        value, held = lax.optimization_barrier((value, last))
        if self.far:
            self.far = held
        else:
            self.behind[-1], self.ahead[-1] = held
        return value

    def blocks(self):
        return jnp.concatenate(self.ahead + self.far + self.behind[:0:-1], axis=0)


def take_rows(value, index):
    return value.at[index].get(mode="promise_in_bounds")


def body(
    tokens, route_ids, route_weights, train_map, serve_place, train_gate, train_up, train_down
):
    plane = lax.axis_index("z")
    line = lax.axis_index(XC)
    quarter = lax.axis_index("y")
    slot_count = serve_place.shape[0]
    part_count = slot_count // EXPERTS
    piece_rows = train_gate.shape[1]
    width = train_gate.shape[2]
    block_rows = piece_rows // PLANE
    steps, tok_count, model_width = tokens.shape
    out_width = model_width // Y
    own_tokens = steps * tok_count
    line_tokens = own_tokens * Z
    capacity = Z * steps * MOST // 2

    slot_iota = jnp.arange(slot_count, dtype=jnp.int32)
    inverse = jnp.sum(
        jnp.where(train_map[:, None] == slot_iota[None, :], slot_iota[:, None], 0), axis=0
    )
    relative = (inverse - plane * PLANE + slot_count) % slot_count
    place_rank = jnp.sum(
        (serve_place[:, None] == serve_place[None, :])
        & (slot_iota[None, :] < slot_iota[:, None]),
        axis=1,
    )
    near_experts = lax.dynamic_slice(serve_place, (plane * PLANE,), (PLANE,))
    near_rank = lax.dynamic_slice(place_rank, (plane * PLANE,), (PLANE,))
    near_count = jnp.sum(near_experts[:, None] == serve_place[None, :], axis=1)
    wanted = near_experts[:, None] * part_count + jnp.arange(part_count, dtype=jnp.int32)[None, :]
    chosen = take_rows(relative, wanted)

    def spread(piece):
        return exchange(piece.reshape(PLANE, block_rows, width), XC)

    def pick(ring):
        return take_rows(ring.blocks(), chosen)

    def assemble(arrived):
        return jnp.swapaxes(arrived, 0, 1).reshape(1, part_count * piece_rows, width)

    gate_ring = Ring(spread(train_gate))
    train_up = gate_ring.hold(train_up)
    block_up = spread(train_up)
    gate_ring.hop()
    tokens, block_up, train_down = gate_ring.hold((tokens, block_up, train_down))

    experts = jnp.arange(EXPERTS, dtype=jnp.int32)
    hot = route_ids.reshape(own_tokens, -1)[:, :, None] == experts
    named = jnp.any(hot, axis=1).astype(jnp.bfloat16)
    weight = jnp.sum(
        jnp.where(hot, route_weights.reshape(own_tokens, -1)[:, :, None], 0.0), axis=1
    )
    high = weight.astype(jnp.bfloat16)
    rest = weight - high.astype(jnp.float32)
    middle = rest.astype(jnp.bfloat16)
    low = (rest - middle.astype(jnp.float32)).astype(jnp.bfloat16)
    own_rows = lax.dynamic_slice(
        tokens.reshape(own_tokens, model_width),
        (0, quarter * out_width),
        (own_tokens, out_width),
    )
    own_block = jnp.concatenate([own_rows, named, high, middle, low], axis=1)
    line_block = exchange(jnp.broadcast_to(own_block, (Z,) + own_block.shape), "z")
    gate_ring.hop()
    line_block = gate_ring.hold(line_block).reshape(line_tokens, -1)
    line_rows = line_block[:, :out_width]
    line_routes = line_block[:, out_width:]
    token_iota = jnp.arange(line_tokens, dtype=jnp.int32)
    earlier = (token_iota[None, :] < token_iota[:, None]).astype(jnp.bfloat16)
    near_hot = near_experts[:, None] == experts[None, :]

    def place(routes, line_index):
        names = routes[..., :EXPERTS]
        seen = jnp.einsum("ut,lte->lue", earlier, names, preferred_element_type=jnp.float32)

        def of_near(table):
            return jnp.sum(
                jnp.where(near_hot[None, :, None, :], table.astype(jnp.float32)[:, None], 0.0), axis=3
            )

        near_seen = of_near(seen).astype(jnp.int32)
        turn = (near_seen + line_index[:, None, None]) % near_count[None, :, None]
        position = near_seen // near_count[None, :, None]
        sent = (of_near(names) > 0.5) & (turn == near_rank[None, :, None])
        rows = jnp.arange(capacity, dtype=jnp.int32)[None, None, :, None]
        return sent[:, :, None, :] & (position[:, :, None, :] == rows)

    own_placing = place(line_routes[None], line[None])[0].astype(jnp.bfloat16)
    send_rows = jnp.einsum(
        "spt,td->spd", own_placing, line_rows, preferred_element_type=jnp.float32
    ).astype(jnp.bfloat16)
    route_rows = line_routes.reshape(-1, out_width)
    send_rows = jnp.concatenate(
        [send_rows, jnp.broadcast_to(route_rows, (PLANE,) + route_rows.shape)], axis=1
    )
    received = exchange(send_rows, XC)
    gate_ring.hop()
    received, train_down = gate_ring.hold((received, train_down))
    block_down = spread(train_down)
    gate_ring.hop()
    block_down = gate_ring.hold(block_down)
    inputs = lax.all_gather(
        received[:, :capacity].reshape(PLANE * capacity, out_width), "y", axis=0, tiled=False
    )
    routes = received[:, capacity:].reshape(PLANE, line_tokens, -1)
    placing = place(routes, jnp.arange(PLANE, dtype=jnp.int32))
    weights = sum(
        routes[..., k * EXPERTS : (k + 1) * EXPERTS].astype(jnp.float32) for k in (1, 2, 3)
    )
    own_expert = lax.dynamic_slice(near_experts, (line,), (1,))
    own_weight = jnp.sum(jnp.where(experts == own_expert, weights, 0.0), axis=2)
    own_sent = lax.dynamic_slice(
        placing, (0, line, 0, 0), (PLANE, 1, capacity, line_tokens)
    )[:, 0]
    row_weight = jnp.sum(jnp.where(own_sent, own_weight[:, None, :], 0.0), axis=2)
    placing = placing.astype(jnp.bfloat16)

    up_ring = Ring(block_up).hop()
    arrived_gate = exchange(pick(gate_ring), XC)
    up_ring.hop().hop()
    arrived_gate = up_ring.hold(arrived_gate)
    up_ring.hop()
    serve_gate = assemble(arrived_gate)
    down_ring = Ring(block_down).hop()
    arrived_up = exchange(pick(up_ring), XC)
    down_ring.hop()
    inputs, arrived_up = down_ring.hold((inputs, arrived_up))
    down_ring.hop()
    serve_up = assemble(arrived_up)
    by_part = (part_count, piece_rows, width)
    gate_act = jnp.einsum(
        "ymd,ydf->mf", inputs, serve_gate.reshape(by_part), preferred_element_type=jnp.float32
    )
    up_act = jnp.einsum(
        "ymd,ydf->mf", inputs, serve_up.reshape(by_part), preferred_element_type=jnp.float32
    )
    hidden = (jax.nn.silu(gate_act) * up_act * row_weight.reshape(-1, 1)).astype(jnp.bfloat16)

    hidden = down_ring.hold(hidden)
    down_ring.hop()

    plane_hidden = lax.all_gather(hidden, XC, axis=0, tiled=False).reshape(
        PLANE, PLANE, capacity, width
    )
    down_rows = pick(down_ring)
    serve_down = assemble(exchange(down_rows, XC))
    partial_value = jnp.einsum(
        "slpf,syrf->slpyr", plane_hidden, down_rows, preferred_element_type=jnp.float32
    ).astype(jnp.bfloat16)
    plane_out = jnp.einsum(
        "lspt,slpyr->yltr", placing, partial_value, preferred_element_type=jnp.float32
    ).astype(jnp.bfloat16)
    line_out = lax.psum_scatter(
        plane_out.reshape(-1, block_rows), "y", scatter_dimension=0, tiled=True
    )
    home = exchange(
        jnp.swapaxes(line_out.reshape(PLANE, Z, own_tokens, block_rows), 0, 1).reshape(
            Z * PLANE, own_tokens, block_rows
        ),
        EP,
    )
    total = jnp.sum(
        home.reshape(Z, PLANE, own_tokens, block_rows).astype(jnp.float32), axis=0
    ).astype(jnp.bfloat16)
    moe_out = jnp.swapaxes(total, 0, 1).reshape(steps, tok_count, out_width)
    return (serve_gate, serve_up, serve_down, moe_out)


def solution(mesh):
    fine = Mesh(mesh.devices.reshape(Z, X, C, Y), ("z", "x", "c", "y"))
    in_specs = (
        P(None, EP, None),
        P(None, EP, None),
        P(None, EP, None),
        P(),
        P(),
        P(EP, None, "y"),
        P(EP, None, "y"),
        P(EP, None, "y"),
    )
    out_specs = (P(EP, None, "y"), P(EP, None, "y"), P(EP, None, "y"), P(None, EP, "y"))
    return jax.shard_map(body, mesh=fine, in_specs=in_specs, out_specs=out_specs, check_vma=False)
```

```python
import jax
import jax.numpy as jnp
from jax import lax
from jax.experimental import pallas as pl
from jax.experimental.pallas import tpu as pltpu
from jax.sharding import Mesh, PartitionSpec as P

EXPERTS = 16
MOST = 10
Z, X, C, Y = 8, 4, 2, 4
PLANE = X * C
EP = ("z", "x", "c")
XC = ("x", "c")


def exchange(value, axes):
    return lax.all_to_all(value, axes, split_axis=0, concat_axis=0, tiled=True)


def shift(value, step):
    return lax.ppermute(value, "z", [(i, (i + step) % Z) for i in range(Z)])


class Ring:
    def __init__(self, block):
        self.ahead = [block]
        self.behind = [block]
        self.far = []

    def hop(self):
        if len(self.ahead) < Z // 2:
            self.behind.append(shift(self.behind[-1], 1))
            self.ahead.append(shift(self.ahead[-1], -1))
        else:
            half = self.ahead[0].shape[0] // 2
            self.far = [shift(self.behind[-1][:half], 1), shift(self.ahead[-1][half:], -1)]
        return self

    def hold(self, value):
        last = self.far or [self.behind[-1], self.ahead[-1]]
        value, held = lax.optimization_barrier((value, last))
        if self.far:
            self.far = held
        else:
            self.behind[-1], self.ahead[-1] = held
        return value

    def pick(self, index):
        blocks = self.ahead + self.far + self.behind[:0:-1]
        return pick_pieces(index.reshape(-1), blocks)


def pick_kernel(index_ref, *refs):
    blocks, out_ref, sems = refs[:-2], refs[-2], refs[-1]
    count = out_ref.shape[0]
    half = blocks[Z // 2].shape[0]

    def start(i, carry):
        distance = index_ref[i] >> 4
        place = index_ref[i] & 15

        def copy(block, piece):
            pltpu.make_async_copy(block.at[piece], out_ref.at[i], sems.at[i]).start()

        for k in range(Z):
            if k == Z // 2:
                pl.when((distance == k) & (place < half))(lambda: copy(blocks[Z // 2], place))
                pl.when((distance == k) & (place >= half))(
                    lambda: copy(blocks[Z // 2 + 1], place - half)
                )
            else:
                block = blocks[k if k < Z // 2 else k + 1]
                pl.when(distance == k)(lambda block=block: copy(block, place))
        return carry

    def finish(i, carry):
        pltpu.make_async_copy(blocks[0].at[0], out_ref.at[i], sems.at[i]).wait()
        return carry

    lax.fori_loop(0, count, start, 0)
    lax.fori_loop(0, count, finish, 0)


def pick_pieces(index, blocks):
    count = index.shape[0]
    return pl.pallas_call(
        pick_kernel,
        out_shape=jax.ShapeDtypeStruct((count,) + blocks[0].shape[1:], blocks[0].dtype),
        in_specs=[pl.BlockSpec(memory_space=pltpu.SMEM)]
        + [pl.BlockSpec(memory_space=pl.ANY)] * len(blocks),
        out_specs=pl.BlockSpec(memory_space=pl.ANY),
        scratch_shapes=[pltpu.SemaphoreType.DMA((count,))],
        name="pick_pieces",
    )(index, *blocks)


def take_rows(value, index):
    return value.at[index].get(mode="promise_in_bounds")


def body(
    tokens, route_ids, route_weights, train_map, serve_place, train_gate, train_up, train_down
):
    plane = lax.axis_index("z")
    line = lax.axis_index(XC)
    quarter = lax.axis_index("y")
    slot_count = serve_place.shape[0]
    part_count = slot_count // EXPERTS
    piece_rows = train_gate.shape[1]
    width = train_gate.shape[2]
    block_rows = piece_rows // PLANE
    steps, tok_count, model_width = tokens.shape
    out_width = model_width // Y
    own_tokens = steps * tok_count
    line_tokens = own_tokens * Z
    capacity = Z * steps * MOST // 2

    slot_iota = jnp.arange(slot_count, dtype=jnp.int32)
    inverse = jnp.sum(
        jnp.where(train_map[:, None] == slot_iota[None, :], slot_iota[:, None], 0), axis=0
    )
    relative = (inverse - plane * PLANE + slot_count) % slot_count
    place_rank = jnp.sum(
        (serve_place[:, None] == serve_place[None, :])
        & (slot_iota[None, :] < slot_iota[:, None]),
        axis=1,
    )
    near_experts = lax.dynamic_slice(serve_place, (plane * PLANE,), (PLANE,))
    near_rank = lax.dynamic_slice(place_rank, (plane * PLANE,), (PLANE,))
    near_count = jnp.sum(near_experts[:, None] == serve_place[None, :], axis=1)
    wanted = near_experts[:, None] * part_count + jnp.arange(part_count, dtype=jnp.int32)[None, :]
    chosen = take_rows(relative // PLANE * 16 + relative % PLANE, wanted)

    def spread(piece):
        return exchange(piece.reshape(PLANE, block_rows, width), XC)

    def pick(ring):
        return ring.pick(chosen).reshape(PLANE, part_count, block_rows, width)

    def assemble(arrived):
        return jnp.swapaxes(arrived, 0, 1).reshape(1, part_count * piece_rows, width)

    experts = jnp.arange(EXPERTS, dtype=jnp.int32)
    hot = route_ids.reshape(own_tokens, -1)[:, :, None] == experts
    named = jnp.any(hot, axis=1).astype(jnp.bfloat16)
    weight = jnp.sum(
        jnp.where(hot, route_weights.reshape(own_tokens, -1)[:, :, None], 0.0), axis=1
    )
    high = weight.astype(jnp.bfloat16)
    rest = weight - high.astype(jnp.float32)
    middle = rest.astype(jnp.bfloat16)
    low = (rest - middle.astype(jnp.float32)).astype(jnp.bfloat16)
    own_rows = lax.dynamic_slice(
        tokens.reshape(own_tokens, model_width),
        (0, quarter * out_width),
        (own_tokens, out_width),
    )
    own_block = jnp.concatenate([own_rows, named, high, middle, low], axis=1)
    spare = block_rows * width // own_tokens - own_block.shape[1]
    own_block = jnp.pad(own_block, ((0, 0), (0, spare))).reshape(1, block_rows, width)
    block_gate = spread(train_gate)
    block_gate, train_up = lax.optimization_barrier((block_gate, train_up))
    block_up = spread(train_up)
    gate_ring = Ring(jnp.concatenate([block_gate, own_block], axis=0)).hop()
    block_up = gate_ring.hold(block_up)
    gate_ring.hop()
    train_down = gate_ring.hold(train_down)
    block_down = spread(train_down)
    gate_ring.hop()
    block_down = gate_ring.hold(block_down)
    gate_ring.hop()
    up_ring = Ring(block_up).hop()

    planes = jnp.arange(Z, dtype=jnp.int32)
    line_block = gate_ring.pick((planes - plane + Z) % Z * 16 + PLANE)
    line_block = line_block.reshape(line_tokens, -1)
    line_rows = line_block[:, :out_width]
    line_routes = line_block[:, out_width : out_width + 4 * EXPERTS]
    token_iota = jnp.arange(line_tokens, dtype=jnp.int32)
    earlier = (token_iota[None, :] < token_iota[:, None]).astype(jnp.bfloat16)
    near_hot = near_experts[:, None] == experts[None, :]

    def place(routes, line_index):
        names = routes[..., :EXPERTS]
        seen = jnp.einsum("ut,lte->lue", earlier, names, preferred_element_type=jnp.float32)

        def of_near(table):
            return jnp.sum(
                jnp.where(near_hot[None, :, None, :], table.astype(jnp.float32)[:, None], 0.0), axis=3
            )

        near_seen = of_near(seen).astype(jnp.int32)
        turn = (near_seen + line_index[:, None, None]) % near_count[None, :, None]
        position = near_seen // near_count[None, :, None]
        sent = (of_near(names) > 0.5) & (turn == near_rank[None, :, None])
        rows = jnp.arange(capacity, dtype=jnp.int32)[None, None, :, None]
        return sent[:, :, None, :] & (position[:, :, None, :] == rows)

    own_placing = place(line_routes[None], line[None])[0].astype(jnp.bfloat16)
    send_rows = jnp.einsum(
        "spt,td->spd", own_placing, line_rows, preferred_element_type=jnp.float32
    ).astype(jnp.bfloat16)
    route_rows = line_routes.reshape(-1, out_width)
    send_rows = jnp.concatenate(
        [send_rows, jnp.broadcast_to(route_rows, (PLANE,) + route_rows.shape)], axis=1
    )
    received = up_ring.hold(exchange(send_rows, XC))
    inputs = lax.all_gather(
        received[:, :capacity].reshape(PLANE * capacity, out_width), "y", axis=0, tiled=False
    )
    routes = received[:, capacity:].reshape(PLANE, line_tokens, -1)
    placing = place(routes, jnp.arange(PLANE, dtype=jnp.int32))
    weights = sum(
        routes[..., k * EXPERTS : (k + 1) * EXPERTS].astype(jnp.float32) for k in (1, 2, 3)
    )
    own_expert = lax.dynamic_slice(near_experts, (line,), (1,))
    own_weight = jnp.sum(jnp.where(experts == own_expert, weights, 0.0), axis=2)
    own_sent = lax.dynamic_slice(
        placing, (0, line, 0, 0), (PLANE, 1, capacity, line_tokens)
    )[:, 0]
    row_weight = jnp.sum(jnp.where(own_sent, own_weight[:, None, :], 0.0), axis=2)
    placing = placing.astype(jnp.bfloat16)

    gate_ring.far = up_ring.hold(gate_ring.far)
    arrived_gate = exchange(pick(gate_ring), XC)
    up_ring.hop().hop()
    arrived_gate = up_ring.hold(arrived_gate)
    up_ring.hop()
    serve_gate = assemble(arrived_gate)
    down_ring = Ring(block_down).hop()
    arrived_up = exchange(pick(up_ring), XC)
    down_ring.hop()
    inputs, arrived_up = down_ring.hold((inputs, arrived_up))
    down_ring.hop()
    serve_up = assemble(arrived_up)
    by_part = (part_count, piece_rows, width)
    gate_act = jnp.einsum(
        "ymd,ydf->mf", inputs, serve_gate.reshape(by_part), preferred_element_type=jnp.float32
    )
    up_act = jnp.einsum(
        "ymd,ydf->mf", inputs, serve_up.reshape(by_part), preferred_element_type=jnp.float32
    )
    hidden = (jax.nn.silu(gate_act) * up_act * row_weight.reshape(-1, 1)).astype(jnp.bfloat16)

    hidden = down_ring.hold(hidden)
    down_ring.hop()

    plane_hidden = lax.all_gather(hidden, XC, axis=0, tiled=False).reshape(
        PLANE, PLANE, capacity, width
    )
    down_rows = pick(down_ring)
    serve_down = assemble(exchange(down_rows, XC))
    partial_value = jnp.einsum(
        "slpf,syrf->slpyr", plane_hidden, down_rows, preferred_element_type=jnp.float32
    ).astype(jnp.bfloat16)
    plane_out = jnp.einsum(
        "lspt,slpyr->yltr", placing, partial_value, preferred_element_type=jnp.float32
    ).astype(jnp.bfloat16)
    line_out = lax.psum_scatter(
        plane_out.reshape(-1, block_rows), "y", scatter_dimension=0, tiled=True
    )
    home = exchange(
        jnp.swapaxes(line_out.reshape(PLANE, Z, own_tokens, block_rows), 0, 1).reshape(
            Z * PLANE, own_tokens, block_rows
        ),
        EP,
    )
    total = jnp.sum(
        home.reshape(Z, PLANE, own_tokens, block_rows).astype(jnp.float32), axis=0
    ).astype(jnp.bfloat16)
    moe_out = jnp.swapaxes(total, 0, 1).reshape(steps, tok_count, out_width)
    return (serve_gate, serve_up, serve_down, moe_out)


def solution(mesh):
    fine = Mesh(mesh.devices.reshape(Z, X, C, Y), ("z", "x", "c", "y"))
    in_specs = (
        P(None, EP, None),
        P(None, EP, None),
        P(None, EP, None),
        P(),
        P(),
        P(EP, None, "y"),
        P(EP, None, "y"),
        P(EP, None, "y"),
    )
    out_specs = (P(EP, None, "y"), P(EP, None, "y"), P(EP, None, "y"), P(None, EP, "y"))
    return jax.shard_map(body, mesh=fine, in_specs=in_specs, out_specs=out_specs, check_vma=False)
```

```python
import jax
import jax.numpy as jnp
from jax import lax
from jax.experimental import pallas as pl
from jax.experimental.pallas import tpu as pltpu
from jax.sharding import Mesh, PartitionSpec as P

EXPERTS = 16
MOST = 10
Z, X, C, Y = 8, 4, 2, 4
PLANE = X * C
EP = ("z", "x", "c")
XC = ("x", "c")


def exchange(value, axes):
    return lax.all_to_all(value, axes, split_axis=0, concat_axis=0, tiled=True)


def shift(value, step):
    return lax.ppermute(value, "z", [(i, (i + step) % Z) for i in range(Z)])


class Ring:
    def __init__(self, block):
        self.ahead = [block]
        self.behind = [block]
        self.far = []

    def hop(self):
        if len(self.ahead) < Z // 2:
            self.behind.append(shift(self.behind[-1], 1))
            self.ahead.append(shift(self.ahead[-1], -1))
        else:
            half = self.ahead[0].shape[0] // 2
            self.far = [shift(self.behind[-1][:half], 1), shift(self.ahead[-1][half:], -1)]
        return self

    def hold(self, value):
        last = self.far or [self.behind[-1], self.ahead[-1]]
        value, held = lax.optimization_barrier((value, last))
        if self.far:
            self.far = held
        else:
            self.behind[-1], self.ahead[-1] = held
        return value

    def pick(self, index):
        blocks = self.ahead + self.far + self.behind[:0:-1]
        return pick_pieces(index.reshape(-1), blocks)


def pick_kernel(index_ref, *refs):
    blocks, out_ref, held_ref, read_sems, write_sems = refs[:-4], *refs[-4:]
    count = out_ref.shape[0]
    half = blocks[Z // 2].shape[0]

    def read(i, carry):
        distance = index_ref[i] >> 4
        place = index_ref[i] & 15

        def copy(block, piece):
            pltpu.make_async_copy(block.at[piece], held_ref.at[i], read_sems.at[i]).start()

        for k in range(Z):
            if k == Z // 2:
                pl.when((distance == k) & (place < half))(lambda: copy(blocks[Z // 2], place))
                pl.when((distance == k) & (place >= half))(
                    lambda: copy(blocks[Z // 2 + 1], place - half)
                )
            else:
                block = blocks[k if k < Z // 2 else k + 1]
                pl.when(distance == k)(lambda block=block: copy(block, place))
        return carry

    def write(i, carry):
        pltpu.make_async_copy(blocks[0].at[0], held_ref.at[i], read_sems.at[i]).wait()
        pltpu.make_async_copy(held_ref.at[i], out_ref.at[i], write_sems.at[i]).start()
        return carry

    def finish(i, carry):
        pltpu.make_async_copy(held_ref.at[i], out_ref.at[i], write_sems.at[i]).wait()
        return carry

    lax.fori_loop(0, count, read, 0)
    lax.fori_loop(0, count, write, 0)
    lax.fori_loop(0, count, finish, 0)


def pick_pieces(index, blocks):
    count = index.shape[0]
    shape = (count,) + blocks[0].shape[1:]
    return pl.pallas_call(
        pick_kernel,
        out_shape=jax.ShapeDtypeStruct(shape, blocks[0].dtype),
        in_specs=[pl.BlockSpec(memory_space=pltpu.SMEM)]
        + [pl.BlockSpec(memory_space=pl.ANY)] * len(blocks),
        out_specs=pl.BlockSpec(memory_space=pl.ANY),
        scratch_shapes=[
            pltpu.VMEM(shape, blocks[0].dtype),
            pltpu.SemaphoreType.DMA((count,)),
            pltpu.SemaphoreType.DMA((count,)),
        ],
        name="pick_pieces",
    )(index, *blocks)


def take_rows(value, index):
    return value.at[index].get(mode="promise_in_bounds")


def body(
    tokens, route_ids, route_weights, train_map, serve_place, train_gate, train_up, train_down
):
    plane = lax.axis_index("z")
    line = lax.axis_index(XC)
    quarter = lax.axis_index("y")
    slot_count = serve_place.shape[0]
    part_count = slot_count // EXPERTS
    piece_rows = train_gate.shape[1]
    width = train_gate.shape[2]
    block_rows = piece_rows // PLANE
    steps, tok_count, model_width = tokens.shape
    out_width = model_width // Y
    own_tokens = steps * tok_count
    line_tokens = own_tokens * Z
    capacity = Z * steps * MOST // 2

    slot_iota = jnp.arange(slot_count, dtype=jnp.int32)
    inverse = jnp.sum(
        jnp.where(train_map[:, None] == slot_iota[None, :], slot_iota[:, None], 0), axis=0
    )
    relative = (inverse - plane * PLANE + slot_count) % slot_count
    place_rank = jnp.sum(
        (serve_place[:, None] == serve_place[None, :])
        & (slot_iota[None, :] < slot_iota[:, None]),
        axis=1,
    )
    near_experts = lax.dynamic_slice(serve_place, (plane * PLANE,), (PLANE,))
    near_rank = lax.dynamic_slice(place_rank, (plane * PLANE,), (PLANE,))
    near_count = jnp.sum(near_experts[:, None] == serve_place[None, :], axis=1)
    wanted = near_experts[:, None] * part_count + jnp.arange(part_count, dtype=jnp.int32)[None, :]
    chosen = take_rows(relative // PLANE * 16 + relative % PLANE, wanted)

    def spread(piece):
        return exchange(piece.reshape(PLANE, block_rows, width), XC)

    def pick(ring):
        return ring.pick(chosen).reshape(PLANE, part_count, block_rows, width)

    def assemble(arrived):
        return jnp.swapaxes(arrived, 0, 1).reshape(1, part_count * piece_rows, width)

    experts = jnp.arange(EXPERTS, dtype=jnp.int32)
    hot = route_ids.reshape(own_tokens, -1)[:, :, None] == experts
    named = jnp.any(hot, axis=1).astype(jnp.bfloat16)
    weight = jnp.sum(
        jnp.where(hot, route_weights.reshape(own_tokens, -1)[:, :, None], 0.0), axis=1
    )
    high = weight.astype(jnp.bfloat16)
    rest = weight - high.astype(jnp.float32)
    middle = rest.astype(jnp.bfloat16)
    low = (rest - middle.astype(jnp.float32)).astype(jnp.bfloat16)
    own_rows = lax.dynamic_slice(
        tokens.reshape(own_tokens, model_width),
        (0, quarter * out_width),
        (own_tokens, out_width),
    )
    own_block = jnp.concatenate([own_rows, named, high, middle, low], axis=1)
    spare = block_rows * width // own_tokens - own_block.shape[1]
    own_block = jnp.pad(own_block, ((0, 0), (0, spare))).reshape(1, block_rows, width)
    block_gate = spread(train_gate)
    block_gate, train_up = lax.optimization_barrier((block_gate, train_up))
    block_up = spread(train_up)
    gate_ring = Ring(jnp.concatenate([block_gate, own_block], axis=0)).hop()
    block_up = gate_ring.hold(block_up)
    gate_ring.hop()
    train_down = gate_ring.hold(train_down)
    block_down = spread(train_down)
    gate_ring.hop()
    block_down = gate_ring.hold(block_down)
    gate_ring.hop()
    up_ring = Ring(block_up).hop()

    planes = jnp.arange(Z, dtype=jnp.int32)
    line_block = gate_ring.pick((planes - plane + Z) % Z * 16 + PLANE)
    line_block = line_block.reshape(line_tokens, -1)
    line_rows = line_block[:, :out_width]
    line_routes = line_block[:, out_width : out_width + 4 * EXPERTS]
    token_iota = jnp.arange(line_tokens, dtype=jnp.int32)
    earlier = (token_iota[None, :] < token_iota[:, None]).astype(jnp.bfloat16)
    near_hot = near_experts[:, None] == experts[None, :]

    def place(routes, line_index):
        names = routes[..., :EXPERTS]
        seen = jnp.einsum("ut,lte->lue", earlier, names, preferred_element_type=jnp.float32)

        def of_near(table):
            return jnp.sum(
                jnp.where(near_hot[None, :, None, :], table.astype(jnp.float32)[:, None], 0.0), axis=3
            )

        near_seen = of_near(seen).astype(jnp.int32)
        turn = (near_seen + line_index[:, None, None]) % near_count[None, :, None]
        position = near_seen // near_count[None, :, None]
        sent = (of_near(names) > 0.5) & (turn == near_rank[None, :, None])
        rows = jnp.arange(capacity, dtype=jnp.int32)[None, None, :, None]
        return sent[:, :, None, :] & (position[:, :, None, :] == rows)

    own_placing = place(line_routes[None], line[None])[0].astype(jnp.bfloat16)
    send_rows = jnp.einsum(
        "spt,td->spd", own_placing, line_rows, preferred_element_type=jnp.float32
    ).astype(jnp.bfloat16)
    route_rows = line_routes.reshape(-1, out_width)
    send_rows = jnp.concatenate(
        [send_rows, jnp.broadcast_to(route_rows, (PLANE,) + route_rows.shape)], axis=1
    )
    received = up_ring.hold(exchange(send_rows, XC))
    inputs = lax.all_gather(
        received[:, :capacity].reshape(PLANE * capacity, out_width), "y", axis=0, tiled=False
    )
    routes = received[:, capacity:].reshape(PLANE, line_tokens, -1)
    placing = place(routes, jnp.arange(PLANE, dtype=jnp.int32))
    weights = sum(
        routes[..., k * EXPERTS : (k + 1) * EXPERTS].astype(jnp.float32) for k in (1, 2, 3)
    )
    own_expert = lax.dynamic_slice(near_experts, (line,), (1,))
    own_weight = jnp.sum(jnp.where(experts == own_expert, weights, 0.0), axis=2)
    own_sent = lax.dynamic_slice(
        placing, (0, line, 0, 0), (PLANE, 1, capacity, line_tokens)
    )[:, 0]
    row_weight = jnp.sum(jnp.where(own_sent, own_weight[:, None, :], 0.0), axis=2)
    placing = placing.astype(jnp.bfloat16)

    gate_ring.far = up_ring.hold(gate_ring.far)
    arrived_gate = exchange(pick(gate_ring), XC)
    up_ring.hop().hop()
    arrived_gate = up_ring.hold(arrived_gate)
    up_ring.hop()
    serve_gate = assemble(arrived_gate)
    down_ring = Ring(block_down).hop()
    arrived_up = exchange(pick(up_ring), XC)
    down_ring.hop()
    inputs, arrived_up = down_ring.hold((inputs, arrived_up))
    down_ring.hop()
    serve_up = assemble(arrived_up)
    by_part = (part_count, piece_rows, width)
    gate_act = jnp.einsum(
        "ymd,ydf->mf", inputs, serve_gate.reshape(by_part), preferred_element_type=jnp.float32
    )
    up_act = jnp.einsum(
        "ymd,ydf->mf", inputs, serve_up.reshape(by_part), preferred_element_type=jnp.float32
    )
    hidden = (jax.nn.silu(gate_act) * up_act * row_weight.reshape(-1, 1)).astype(jnp.bfloat16)

    hidden = down_ring.hold(hidden)
    down_ring.hop()

    plane_hidden = lax.all_gather(hidden, XC, axis=0, tiled=False).reshape(
        PLANE, PLANE, capacity, width
    )
    down_rows = pick(down_ring)
    serve_down = assemble(exchange(down_rows, XC))
    partial_value = jnp.einsum(
        "slpf,syrf->slpyr", plane_hidden, down_rows, preferred_element_type=jnp.float32
    ).astype(jnp.bfloat16)
    plane_out = jnp.einsum(
        "lspt,slpyr->yltr", placing, partial_value, preferred_element_type=jnp.float32
    ).astype(jnp.bfloat16)
    line_out = lax.psum_scatter(
        plane_out.reshape(-1, block_rows), "y", scatter_dimension=0, tiled=True
    )
    home = exchange(
        jnp.swapaxes(line_out.reshape(PLANE, Z, own_tokens, block_rows), 0, 1).reshape(
            Z * PLANE, own_tokens, block_rows
        ),
        EP,
    )
    total = jnp.sum(
        home.reshape(Z, PLANE, own_tokens, block_rows).astype(jnp.float32), axis=0
    ).astype(jnp.bfloat16)
    moe_out = jnp.swapaxes(total, 0, 1).reshape(steps, tok_count, out_width)
    return (serve_gate, serve_up, serve_down, moe_out)


def solution(mesh):
    fine = Mesh(mesh.devices.reshape(Z, X, C, Y), ("z", "x", "c", "y"))
    in_specs = (
        P(None, EP, None),
        P(None, EP, None),
        P(None, EP, None),
        P(),
        P(),
        P(EP, None, "y"),
        P(EP, None, "y"),
        P(EP, None, "y"),
    )
    out_specs = (P(EP, None, "y"), P(EP, None, "y"), P(EP, None, "y"), P(None, EP, "y"))
    return jax.shard_map(body, mesh=fine, in_specs=in_specs, out_specs=out_specs, check_vma=False)
```

```python
import functools

import jax
import jax.numpy as jnp
from jax import lax
from jax.experimental import pallas as pl
from jax.experimental.pallas import tpu as pltpu
from jax.sharding import Mesh, PartitionSpec as P

EXPERTS = 16
MOST = 10
Z, X, C, Y = 8, 4, 2, 4
PLANE = X * C
EP = ("z", "x", "c")
XC = ("x", "c")


def exchange(value, axes):
    return lax.all_to_all(value, axes, split_axis=0, concat_axis=0, tiled=True)


def shift(value, step):
    return lax.ppermute(value, "z", [(i, (i + step) % Z) for i in range(Z)])


class Ring:
    def __init__(self, block):
        self.ahead = [block]
        self.behind = [block]
        self.far = []
        self.front = [block, block]
        self.places = block.shape[0]

    def hop(self):
        behind, ahead = self.front
        if len(self.ahead) < Z // 2:
            self.front = [shift(behind, 1), shift(ahead, -1)]
            self.behind.append(self.front[0])
            self.ahead.append(self.front[1])
        else:
            half = self.places // 2
            self.far = [shift(behind[:half], 1), shift(ahead[half:], -1)]
        return self

    def hold(self, value):
        last = self.far or [self.behind[-1], self.ahead[-1]]
        value, held = lax.optimization_barrier((value, last))
        if self.far:
            self.far = held
        else:
            self.behind[-1], self.ahead[-1] = held
        return value

    def after(self, *rings):
        for ring in rings:
            self.front = ring.hold(self.front)
        return self

    def blocks(self):
        return self.ahead + self.far + self.behind[:0:-1]


def gather_quarters(block):
    step = [(i, (i + 1) % Y) for i in range(Y)]
    back = [(i, (i - 1) % Y) for i in range(Y)]
    half = block.shape[0] // 2
    before = lax.ppermute(block, "y", step)
    after = lax.ppermute(block, "y", back)
    far = jnp.concatenate(
        [lax.ppermute(before[:half], "y", step), lax.ppermute(after[half:], "y", back)], axis=0
    )
    places = (jnp.arange(Y, dtype=jnp.int32) - lax.axis_index("y") + Y) % Y
    return take_rows(jnp.stack([block, after, far, before]), places)


def pick(index, *rings):
    return pick_pieces(
        index.reshape(-1), tuple(ring.places for ring in rings), [ring.blocks() for ring in rings]
    )


def pick_kernel(places, index_ref, *refs):
    blocks, out_ref, held_ref, read_sems, write_sems = refs[:-4], *refs[-4:]
    count = out_ref.shape[0]

    def split(value, bounds, leaf):
        def part(low, high):
            if high - low == 1:
                leaf(low)
                return
            middle = (low + high) // 2
            pl.when(value < bounds[middle])(lambda: part(low, middle))
            pl.when(value >= bounds[middle])(lambda: part(middle, high))

        part(0, len(bounds) - 1)

    starts = [0]
    for number in places:
        starts.append(starts[-1] + number)

    def read(i, carry):
        distance = index_ref[i] >> 4
        place = index_ref[i] & 15

        def of_ring(ring):
            own = blocks[ring * (Z + 1) : (ring + 1) * (Z + 1)]
            half = starts[ring] + places[ring] // 2

            def copy(block, first):
                pltpu.make_async_copy(
                    block.at[place - first], held_ref.at[i], read_sems.at[i]
                ).start()

            def of_distance(k):
                if k == Z // 2:
                    pl.when(place < half)(lambda: copy(own[k], starts[ring]))
                    pl.when(place >= half)(lambda: copy(own[k + 1], half))
                else:
                    copy(own[k if k < Z // 2 else k + 1], starts[ring])

            split(distance, list(range(Z + 1)), of_distance)

        split(place, starts, of_ring)
        return carry

    def write(i, carry):
        pltpu.make_async_copy(blocks[0].at[0], held_ref.at[i], read_sems.at[i]).wait()
        pltpu.make_async_copy(held_ref.at[i], out_ref.at[i], write_sems.at[i]).start()
        return carry

    def finish(i, carry):
        pltpu.make_async_copy(held_ref.at[i], out_ref.at[i], write_sems.at[i]).wait()
        return carry

    lax.fori_loop(0, count, read, 0)
    lax.fori_loop(0, count, write, 0)
    lax.fori_loop(0, count, finish, 0)


def pick_pieces(index, places, rings):
    count = index.shape[0]
    blocks = sum(rings, [])
    shape = (count,) + blocks[0].shape[1:]
    return pl.pallas_call(
        functools.partial(pick_kernel, places),
        out_shape=jax.ShapeDtypeStruct(shape, blocks[0].dtype),
        in_specs=[pl.BlockSpec(memory_space=pltpu.SMEM)]
        + [pl.BlockSpec(memory_space=pl.ANY)] * len(blocks),
        out_specs=pl.BlockSpec(memory_space=pl.ANY),
        scratch_shapes=[
            pltpu.VMEM(shape, blocks[0].dtype),
            pltpu.SemaphoreType.DMA((count,)),
            pltpu.SemaphoreType.DMA((count,)),
        ],
        name="pick_pieces",
    )(index, *blocks)


def take_rows(value, index):
    return value.at[index].get(mode="promise_in_bounds")


def body(
    tokens, route_ids, route_weights, train_map, serve_place, train_gate, train_up, train_down
):
    plane = lax.axis_index("z")
    line = lax.axis_index(XC)
    quarter = lax.axis_index("y")
    slot_count = serve_place.shape[0]
    part_count = slot_count // EXPERTS
    piece_rows = train_gate.shape[1]
    width = train_gate.shape[2]
    block_rows = piece_rows // PLANE
    steps, tok_count, model_width = tokens.shape
    out_width = model_width // Y
    own_tokens = steps * tok_count
    line_tokens = own_tokens * Z
    capacity = Z * steps * MOST // 2

    slot_iota = jnp.arange(slot_count, dtype=jnp.int32)
    inverse = jnp.sum(
        jnp.where(train_map[:, None] == slot_iota[None, :], slot_iota[:, None], 0), axis=0
    )
    relative = (inverse - plane * PLANE + slot_count) % slot_count
    place_rank = jnp.sum(
        (serve_place[:, None] == serve_place[None, :])
        & (slot_iota[None, :] < slot_iota[:, None]),
        axis=1,
    )
    near_experts = lax.dynamic_slice(serve_place, (plane * PLANE,), (PLANE,))
    near_rank = lax.dynamic_slice(place_rank, (plane * PLANE,), (PLANE,))
    near_count = jnp.sum(near_experts[:, None] == serve_place[None, :], axis=1)
    wanted = near_experts[:, None] * part_count + jnp.arange(part_count, dtype=jnp.int32)[None, :]
    chosen = take_rows(relative // PLANE * 16 + relative % PLANE, wanted)
    chosen_slot = take_rows(inverse, wanted)

    half_rows = piece_rows // 2
    chunk_rows = half_rows // PLANE

    def spread(piece):
        return exchange(piece.reshape(PLANE, -1, width), XC)

    def deliver(*rings):
        picked = pick(chosen, *rings)
        return exchange(picked.reshape((PLANE, part_count) + picked.shape[1:]), XC)

    def gather_planes(block):
        rows = lax.all_gather(block.reshape(-1, width), "z", axis=0, tiled=True)
        return rows.reshape(slot_count, -1, width)

    def assemble(*arrived):
        rows = jnp.stack(arrived, axis=1)
        return jnp.transpose(rows, (2, 1, 0, 3, 4)).reshape(1, part_count * piece_rows, width)

    experts = jnp.arange(EXPERTS, dtype=jnp.int32)
    hot = route_ids.reshape(own_tokens, -1)[:, :, None] == experts
    named = jnp.any(hot, axis=1).astype(jnp.bfloat16)
    weight = jnp.sum(
        jnp.where(hot, route_weights.reshape(own_tokens, -1)[:, :, None], 0.0), axis=1
    )
    high = weight.astype(jnp.bfloat16)
    rest = weight - high.astype(jnp.float32)
    middle = rest.astype(jnp.bfloat16)
    low = (rest - middle.astype(jnp.float32)).astype(jnp.bfloat16)
    own_rows = lax.dynamic_slice(
        tokens.reshape(own_tokens, model_width),
        (0, quarter * out_width),
        (own_tokens, out_width),
    )
    own_block = jnp.concatenate([own_rows, named, high, middle, low], axis=1)
    own_pieces = -(-own_block.size // (chunk_rows * width))
    spare = own_pieces * chunk_rows * width // own_tokens - own_block.shape[1]
    own_block = jnp.pad(own_block, ((0, 0), (0, spare)))
    own_block = own_block.reshape(own_pieces, chunk_rows, width)

    gate_first = spread(train_gate[0, :half_rows])
    gate_first, train_up = lax.optimization_barrier((gate_first, train_up))
    up_block = spread(train_up[0, :half_rows])
    up_block, train_gate = lax.optimization_barrier((up_block, train_gate))
    gate_all = [gather_planes(gate_first), gather_planes(spread(train_gate[0, half_rows:]))]
    up_first = Ring(jnp.concatenate([up_block, own_block], axis=0)).hop()
    up_second, train_down = up_first.hold((train_up[0, half_rows:], train_down))
    up_second = Ring(spread(up_second))
    up_first.hop()
    train_down = up_first.hold(train_down)
    block_down = spread(train_down[0])
    up_first.hop()
    up_second.after(up_first)
    block_down = up_first.hold(block_down)
    up_first.hop()
    up_second.hop()
    up_first.far, gate_all[0] = up_second.hold((up_first.far, gate_all[0]))

    planes = jnp.arange(Z, dtype=jnp.int32)
    extra = jnp.arange(own_pieces, dtype=jnp.int32)
    line_block = pick(((planes - plane + Z) % Z * 16 + PLANE)[:, None] + extra[None, :], up_first)
    line_block = line_block.reshape(line_tokens, -1)
    line_rows = line_block[:, :out_width]
    line_routes = line_block[:, out_width : out_width + 4 * EXPERTS]
    token_iota = jnp.arange(line_tokens, dtype=jnp.int32)
    earlier = (token_iota[None, :] < token_iota[:, None]).astype(jnp.bfloat16)
    near_hot = near_experts[:, None] == experts[None, :]

    def place(routes, line_index):
        names = routes[..., :EXPERTS]
        seen = jnp.einsum("ut,lte->lue", earlier, names, preferred_element_type=jnp.float32)

        def of_near(table):
            return jnp.sum(
                jnp.where(near_hot[None, :, None, :], table.astype(jnp.float32)[:, None], 0.0), axis=3
            )

        near_seen = of_near(seen).astype(jnp.int32)
        turn = (near_seen + line_index[:, None, None]) % near_count[None, :, None]
        position = near_seen // near_count[None, :, None]
        sent = (of_near(names) > 0.5) & (turn == near_rank[None, :, None])
        rows = jnp.arange(capacity, dtype=jnp.int32)[None, None, :, None]
        return sent[:, :, None, :] & (position[:, :, None, :] == rows)

    own_placing = place(line_routes[None], line[None])[0].astype(jnp.bfloat16)
    send_rows = jnp.einsum(
        "spt,td->spd", own_placing, line_rows, preferred_element_type=jnp.float32
    ).astype(jnp.bfloat16)
    route_rows = line_routes.reshape(-1, out_width)
    send_rows = jnp.concatenate(
        [send_rows, jnp.broadcast_to(route_rows, (PLANE,) + route_rows.shape)], axis=1
    )
    up_second.hop()
    received, up_first.far = up_second.hold((exchange(send_rows, XC), up_first.far))
    routes = received[:, capacity:].reshape(PLANE, line_tokens, -1)
    placing = place(routes, jnp.arange(PLANE, dtype=jnp.int32))
    weights = sum(
        routes[..., k * EXPERTS : (k + 1) * EXPERTS].astype(jnp.float32) for k in (1, 2, 3)
    )
    own_expert = lax.dynamic_slice(near_experts, (line,), (1,))
    own_weight = jnp.sum(jnp.where(experts == own_expert, weights, 0.0), axis=2)
    own_sent = lax.dynamic_slice(
        placing, (0, line, 0, 0), (PLANE, 1, capacity, line_tokens)
    )[:, 0]
    row_weight = jnp.sum(jnp.where(own_sent, own_weight[:, None, :], 0.0), axis=2)
    placing = placing.astype(jnp.bfloat16)

    def deliver_gate(rows):
        return exchange(take_rows(rows, chosen_slot), XC)

    inputs = gather_quarters(received[:, :capacity].reshape(PLANE * capacity, out_width))
    up_second.hop()
    arrived_gate = [up_second.hold(deliver_gate(gate_all[0]))]
    arrived_up = [up_second.hold(deliver(up_first))]
    down_ring = Ring(block_down).after(up_second)
    up_second.hop()
    arrived_gate.append(deliver_gate(up_second.hold(gate_all[1])))
    arrived_up.append(deliver(up_second))
    down_ring.hop()
    arrived_up[1], inputs = down_ring.hold((arrived_up[1], inputs))
    down_ring.hop()
    serve_gate = assemble(*arrived_gate)
    serve_up = assemble(*arrived_up)
    by_part = (part_count, piece_rows, width)
    gate_act = jnp.einsum(
        "ymd,ydf->mf", inputs, serve_gate.reshape(by_part), preferred_element_type=jnp.float32
    )
    up_act = jnp.einsum(
        "ymd,ydf->mf", inputs, serve_up.reshape(by_part), preferred_element_type=jnp.float32
    )
    hidden = (jax.nn.silu(gate_act) * up_act * row_weight.reshape(-1, 1)).astype(jnp.bfloat16)

    hidden = down_ring.hold(hidden)
    down_ring.hop().hop()

    plane_hidden = lax.all_gather(hidden, XC, axis=0, tiled=False).reshape(
        PLANE, PLANE, capacity, width
    )
    down_rows = pick(chosen, down_ring).reshape(
        PLANE, part_count, block_rows, width
    )
    serve_down = assemble(exchange(down_rows, XC))
    partial_value = jnp.einsum(
        "slpf,syrf->slpyr", plane_hidden, down_rows, preferred_element_type=jnp.float32
    ).astype(jnp.bfloat16)
    plane_out = jnp.einsum(
        "lspt,slpyr->yltr", placing, partial_value, preferred_element_type=jnp.float32
    ).astype(jnp.bfloat16)
    line_out = lax.psum_scatter(
        plane_out.reshape(-1, block_rows), "y", scatter_dimension=0, tiled=True
    )
    home = exchange(
        jnp.swapaxes(line_out.reshape(PLANE, Z, own_tokens, block_rows), 0, 1).reshape(
            Z * PLANE, own_tokens, block_rows
        ),
        EP,
    )
    total = jnp.sum(
        home.reshape(Z, PLANE, own_tokens, block_rows).astype(jnp.float32), axis=0
    ).astype(jnp.bfloat16)
    moe_out = jnp.swapaxes(total, 0, 1).reshape(steps, tok_count, out_width)
    return (serve_gate, serve_up, serve_down, moe_out)


def solution(mesh):
    fine = Mesh(mesh.devices.reshape(Z, X, C, Y), ("z", "x", "c", "y"))
    in_specs = (
        P(None, EP, None),
        P(None, EP, None),
        P(None, EP, None),
        P(),
        P(),
        P(EP, None, "y"),
        P(EP, None, "y"),
        P(EP, None, "y"),
    )
    out_specs = (P(EP, None, "y"), P(EP, None, "y"), P(EP, None, "y"), P(None, EP, "y"))
    return jax.shard_map(body, mesh=fine, in_specs=in_specs, out_specs=out_specs, check_vma=False)
```

```python
import jax
import jax.numpy as jnp
from jax import lax
from jax.experimental import pallas as pl
from jax.experimental.pallas import tpu as pltpu
from jax.sharding import Mesh, PartitionSpec as P

EXPERTS = 16
MOST = 10
Z, X, C, Y = 8, 4, 2, 4
PLANE = X * C
EP = ("z", "x", "c")
XC = ("x", "c")


def exchange(value, axes):
    return lax.all_to_all(value, axes, split_axis=0, concat_axis=0, tiled=True)


def shift(value, step):
    return lax.ppermute(value, "z", [(i, (i + step) % Z) for i in range(Z)])


class Ring:
    def __init__(self, block):
        self.ahead = [block]
        self.behind = [block]
        self.far = []

    def hop(self):
        if len(self.ahead) < Z // 2:
            self.behind.append(shift(self.behind[-1], 1))
            self.ahead.append(shift(self.ahead[-1], -1))
        else:
            half = self.ahead[0].shape[0] // 2
            self.far = [shift(self.behind[-1][:half], 1), shift(self.ahead[-1][half:], -1)]
        return self

    def hold(self, value):
        last = self.far or [self.behind[-1], self.ahead[-1]]
        value, held = lax.optimization_barrier((value, last))
        if self.far:
            self.far = held
        else:
            self.behind[-1], self.ahead[-1] = held
        return value

    def pick(self, index):
        blocks = self.ahead + self.far + self.behind[:0:-1]
        return pick_pieces(index.reshape(-1), blocks)


def pick_kernel(index_ref, *refs):
    blocks, out_ref, held_ref, read_sems, write_sems = refs[:-4], *refs[-4:]
    count = out_ref.shape[0]
    half = blocks[Z // 2].shape[0]

    def read(i, carry):
        distance = index_ref[i] >> 4
        place = index_ref[i] & 15

        def copy(block, piece):
            pltpu.make_async_copy(block.at[piece], held_ref.at[i], read_sems.at[i]).start()

        for k in range(Z):
            if k == Z // 2:
                pl.when((distance == k) & (place < half))(lambda: copy(blocks[Z // 2], place))
                pl.when((distance == k) & (place >= half))(
                    lambda: copy(blocks[Z // 2 + 1], place - half)
                )
            else:
                block = blocks[k if k < Z // 2 else k + 1]
                pl.when(distance == k)(lambda block=block: copy(block, place))
        return carry

    def write(i, carry):
        pltpu.make_async_copy(blocks[0].at[0], held_ref.at[i], read_sems.at[i]).wait()
        pltpu.make_async_copy(held_ref.at[i], out_ref.at[i], write_sems.at[i]).start()
        return carry

    def finish(i, carry):
        pltpu.make_async_copy(held_ref.at[i], out_ref.at[i], write_sems.at[i]).wait()
        return carry

    lax.fori_loop(0, count, read, 0)
    lax.fori_loop(0, count, write, 0)
    lax.fori_loop(0, count, finish, 0)


def pick_pieces(index, blocks):
    count = index.shape[0]
    shape = (count,) + blocks[0].shape[1:]
    return pl.pallas_call(
        pick_kernel,
        out_shape=jax.ShapeDtypeStruct(shape, blocks[0].dtype),
        in_specs=[pl.BlockSpec(memory_space=pltpu.SMEM)]
        + [pl.BlockSpec(memory_space=pl.ANY)] * len(blocks),
        out_specs=pl.BlockSpec(memory_space=pl.ANY),
        scratch_shapes=[
            pltpu.VMEM(shape, blocks[0].dtype),
            pltpu.SemaphoreType.DMA((count,)),
            pltpu.SemaphoreType.DMA((count,)),
        ],
        name="pick_pieces",
    )(index, *blocks)


def take_rows(value, index):
    return value.at[index].get(mode="promise_in_bounds")


def body(
    tokens, route_ids, route_weights, train_map, serve_place, train_gate, train_up, train_down
):
    plane = lax.axis_index("z")
    line = lax.axis_index(XC)
    quarter = lax.axis_index("y")
    slot_count = serve_place.shape[0]
    part_count = slot_count // EXPERTS
    piece_rows = train_gate.shape[1]
    width = train_gate.shape[2]
    block_rows = piece_rows // PLANE
    steps, tok_count, model_width = tokens.shape
    out_width = model_width // Y
    own_tokens = steps * tok_count
    line_tokens = own_tokens * Z
    capacity = Z * steps * MOST // 2

    slot_iota = jnp.arange(slot_count, dtype=jnp.int32)
    inverse = jnp.sum(
        jnp.where(train_map[:, None] == slot_iota[None, :], slot_iota[:, None], 0), axis=0
    )
    relative = (inverse - plane * PLANE + slot_count) % slot_count
    place_rank = jnp.sum(
        (serve_place[:, None] == serve_place[None, :])
        & (slot_iota[None, :] < slot_iota[:, None]),
        axis=1,
    )
    near_experts = lax.dynamic_slice(serve_place, (plane * PLANE,), (PLANE,))
    near_rank = lax.dynamic_slice(place_rank, (plane * PLANE,), (PLANE,))
    near_count = jnp.sum(near_experts[:, None] == serve_place[None, :], axis=1)
    wanted = near_experts[:, None] * part_count + jnp.arange(part_count, dtype=jnp.int32)[None, :]
    chosen = take_rows(relative // PLANE * 16 + relative % PLANE, wanted)
    chosen_slot = take_rows(inverse, wanted)

    def spread(piece):
        return exchange(piece.reshape(PLANE, block_rows, width), XC)

    def gather_planes(block):
        rows = lax.all_gather(block.reshape(-1, width), "z", axis=0, tiled=True)
        return rows.reshape(slot_count, block_rows, width)

    def assemble(arrived):
        return jnp.swapaxes(arrived, 0, 1).reshape(1, part_count * piece_rows, width)

    experts = jnp.arange(EXPERTS, dtype=jnp.int32)
    hot = route_ids.reshape(own_tokens, -1)[:, :, None] == experts
    named = jnp.any(hot, axis=1).astype(jnp.bfloat16)
    weight = jnp.sum(
        jnp.where(hot, route_weights.reshape(own_tokens, -1)[:, :, None], 0.0), axis=1
    )
    high = weight.astype(jnp.bfloat16)
    rest = weight - high.astype(jnp.float32)
    middle = rest.astype(jnp.bfloat16)
    low = (rest - middle.astype(jnp.float32)).astype(jnp.bfloat16)
    own_rows = lax.dynamic_slice(
        tokens.reshape(own_tokens, model_width),
        (0, quarter * out_width),
        (own_tokens, out_width),
    )
    own_block = jnp.concatenate([own_rows, named, high, middle, low], axis=1)
    block_gate = spread(train_gate)
    block_gate, train_up, own_block = lax.optimization_barrier((block_gate, train_up, own_block))
    gate_all = gather_planes(block_gate)
    block_up = spread(train_up)
    block_up, train_down = lax.optimization_barrier((block_up, train_down))
    up_all = gather_planes(block_up)
    line_block = exchange(jnp.broadcast_to(own_block, (Z,) + own_block.shape), "z")
    line_block, train_down = lax.optimization_barrier((line_block, train_down))
    block_down = spread(train_down)
    line_block = line_block.reshape(line_tokens, -1)
    line_rows = line_block[:, :out_width]
    line_routes = line_block[:, out_width : out_width + 4 * EXPERTS]
    token_iota = jnp.arange(line_tokens, dtype=jnp.int32)
    earlier = (token_iota[None, :] < token_iota[:, None]).astype(jnp.bfloat16)
    near_hot = near_experts[:, None] == experts[None, :]

    def place(routes, line_index):
        names = routes[..., :EXPERTS]
        seen = jnp.einsum("ut,lte->lue", earlier, names, preferred_element_type=jnp.float32)

        def of_near(table):
            return jnp.sum(
                jnp.where(near_hot[None, :, None, :], table.astype(jnp.float32)[:, None], 0.0), axis=3
            )

        near_seen = of_near(seen).astype(jnp.int32)
        turn = (near_seen + line_index[:, None, None]) % near_count[None, :, None]
        position = near_seen // near_count[None, :, None]
        sent = (of_near(names) > 0.5) & (turn == near_rank[None, :, None])
        rows = jnp.arange(capacity, dtype=jnp.int32)[None, None, :, None]
        return sent[:, :, None, :] & (position[:, :, None, :] == rows)

    own_placing = place(line_routes[None], line[None])[0].astype(jnp.bfloat16)
    send_rows = jnp.einsum(
        "spt,td->spd", own_placing, line_rows, preferred_element_type=jnp.float32
    ).astype(jnp.bfloat16)
    route_rows = line_routes.reshape(-1, out_width)
    send_rows = jnp.concatenate(
        [send_rows, jnp.broadcast_to(route_rows, (PLANE,) + route_rows.shape)], axis=1
    )
    received = exchange(send_rows, XC)
    quarters = received[:, :capacity].reshape(PLANE * capacity, out_width)
    half = quarters.shape[0] // 2
    to_next = [(i, (i + 1) % Y) for i in range(Y)]
    to_last = [(i, (i - 1) % Y) for i in range(Y)]
    from_last = lax.ppermute(quarters, "y", to_next)
    from_next = lax.ppermute(quarters, "y", to_last)
    gate_all, from_last, from_next = lax.optimization_barrier((gate_all, from_last, from_next))
    far = [
        lax.ppermute(from_last[:half], "y", to_next),
        lax.ppermute(from_next[half:], "y", to_last),
    ]
    up_all, far, block_down = lax.optimization_barrier((up_all, far, block_down))
    inputs = take_rows(
        jnp.stack([quarters, from_next, jnp.concatenate(far, axis=0), from_last]),
        (jnp.arange(Y, dtype=jnp.int32) - quarter + Y) % Y,
    )
    routes = received[:, capacity:].reshape(PLANE, line_tokens, -1)
    placing = place(routes, jnp.arange(PLANE, dtype=jnp.int32))
    weights = sum(
        routes[..., k * EXPERTS : (k + 1) * EXPERTS].astype(jnp.float32) for k in (1, 2, 3)
    )
    own_expert = lax.dynamic_slice(near_experts, (line,), (1,))
    own_weight = jnp.sum(jnp.where(experts == own_expert, weights, 0.0), axis=2)
    own_sent = lax.dynamic_slice(
        placing, (0, line, 0, 0), (PLANE, 1, capacity, line_tokens)
    )[:, 0]
    row_weight = jnp.sum(jnp.where(own_sent, own_weight[:, None, :], 0.0), axis=2)
    placing = placing.astype(jnp.bfloat16)

    serve_gate = assemble(exchange(take_rows(gate_all, chosen_slot), XC))
    arrived_up = exchange(take_rows(up_all, chosen_slot), XC)
    down_ring = Ring(block_down).hop().hop()
    arrived_up = down_ring.hold(arrived_up)
    down_ring.hop()
    serve_up = assemble(arrived_up)
    by_part = (part_count, piece_rows, width)
    gate_act = jnp.einsum(
        "ymd,ydf->mf", inputs, serve_gate.reshape(by_part), preferred_element_type=jnp.float32
    )
    up_act = jnp.einsum(
        "ymd,ydf->mf", inputs, serve_up.reshape(by_part), preferred_element_type=jnp.float32
    )
    hidden = (jax.nn.silu(gate_act) * up_act * row_weight.reshape(-1, 1)).astype(jnp.bfloat16)

    hidden = down_ring.hold(hidden)
    down_ring.hop()

    plane_hidden = lax.all_gather(hidden, XC, axis=0, tiled=False).reshape(
        PLANE, PLANE, capacity, width
    )
    down_rows = down_ring.pick(chosen).reshape(PLANE, part_count, block_rows, width)
    serve_down = assemble(exchange(down_rows, XC))
    partial_value = jnp.einsum(
        "slpf,syrf->slpyr", plane_hidden, down_rows, preferred_element_type=jnp.float32
    ).astype(jnp.bfloat16)
    plane_out = jnp.einsum(
        "lspt,slpyr->yltr", placing, partial_value, preferred_element_type=jnp.float32
    ).astype(jnp.bfloat16)
    line_out = lax.psum_scatter(
        plane_out.reshape(-1, block_rows), "y", scatter_dimension=0, tiled=True
    )
    home = exchange(
        jnp.swapaxes(line_out.reshape(PLANE, Z, own_tokens, block_rows), 0, 1).reshape(
            Z * PLANE, own_tokens, block_rows
        ),
        EP,
    )
    total = jnp.sum(
        home.reshape(Z, PLANE, own_tokens, block_rows).astype(jnp.float32), axis=0
    ).astype(jnp.bfloat16)
    moe_out = jnp.swapaxes(total, 0, 1).reshape(steps, tok_count, out_width)
    return (serve_gate, serve_up, serve_down, moe_out)


def solution(mesh):
    fine = Mesh(mesh.devices.reshape(Z, X, C, Y), ("z", "x", "c", "y"))
    in_specs = (
        P(None, EP, None),
        P(None, EP, None),
        P(None, EP, None),
        P(),
        P(),
        P(EP, None, "y"),
        P(EP, None, "y"),
        P(EP, None, "y"),
    )
    out_specs = (P(EP, None, "y"), P(EP, None, "y"), P(EP, None, "y"), P(None, EP, "y"))
    return jax.shard_map(body, mesh=fine, in_specs=in_specs, out_specs=out_specs, check_vma=False)
```

```python
import jax
import jax.numpy as jnp
from jax import lax
from jax.experimental import pallas as pl
from jax.experimental.pallas import tpu as pltpu
from jax.sharding import Mesh, PartitionSpec as P

EXPERTS = 16
MOST = 10
Z, X, C, Y = 8, 4, 2, 4
PLANE = X * C
EP = ("z", "x", "c")
XC = ("x", "c")


def exchange(value, axes):
    return lax.all_to_all(value, axes, split_axis=0, concat_axis=0, tiled=True)


def shift(value, step):
    return lax.ppermute(value, "z", [(i, (i + step) % Z) for i in range(Z)])


class Ring:
    def __init__(self, block):
        self.ahead = [block]
        self.behind = [block]
        self.far = []

    def hop(self):
        if len(self.ahead) < Z // 2:
            self.behind.append(shift(self.behind[-1], 1))
            self.ahead.append(shift(self.ahead[-1], -1))
        else:
            half = self.ahead[0].shape[0] // 2
            self.far = [shift(self.behind[-1][:half], 1), shift(self.ahead[-1][half:], -1)]
        return self

    def hold(self, value):
        last = self.far or [self.behind[-1], self.ahead[-1]]
        value, held = lax.optimization_barrier((value, last))
        if self.far:
            self.far = held
        else:
            self.behind[-1], self.ahead[-1] = held
        return value

    def pick(self, index):
        blocks = self.ahead + self.far + self.behind[:0:-1]
        return pick_pieces(index.reshape(-1), blocks)


def pick_kernel(index_ref, *refs):
    blocks, out_ref, held_ref, read_sems, write_sems = refs[:-4], *refs[-4:]
    count = out_ref.shape[0]
    half = blocks[Z // 2].shape[0]

    def read(i, carry):
        distance = index_ref[i] >> 4
        place = index_ref[i] & 15

        def copy(block, piece):
            pltpu.make_async_copy(block.at[piece], held_ref.at[i], read_sems.at[i]).start()

        for k in range(Z):
            if k == Z // 2:
                pl.when((distance == k) & (place < half))(lambda: copy(blocks[Z // 2], place))
                pl.when((distance == k) & (place >= half))(
                    lambda: copy(blocks[Z // 2 + 1], place - half)
                )
            else:
                block = blocks[k if k < Z // 2 else k + 1]
                pl.when(distance == k)(lambda block=block: copy(block, place))
        return carry

    def write(i, carry):
        pltpu.make_async_copy(blocks[0].at[0], held_ref.at[i], read_sems.at[i]).wait()
        pltpu.make_async_copy(held_ref.at[i], out_ref.at[i], write_sems.at[i]).start()
        return carry

    def finish(i, carry):
        pltpu.make_async_copy(held_ref.at[i], out_ref.at[i], write_sems.at[i]).wait()
        return carry

    lax.fori_loop(0, count, read, 0)
    lax.fori_loop(0, count, write, 0)
    lax.fori_loop(0, count, finish, 0)


def pick_pieces(index, blocks):
    count = index.shape[0]
    shape = (count,) + blocks[0].shape[1:]
    return pl.pallas_call(
        pick_kernel,
        out_shape=jax.ShapeDtypeStruct(shape, blocks[0].dtype),
        in_specs=[pl.BlockSpec(memory_space=pltpu.SMEM)]
        + [pl.BlockSpec(memory_space=pl.ANY)] * len(blocks),
        out_specs=pl.BlockSpec(memory_space=pl.ANY),
        scratch_shapes=[
            pltpu.VMEM(shape, blocks[0].dtype),
            pltpu.SemaphoreType.DMA((count,)),
            pltpu.SemaphoreType.DMA((count,)),
        ],
        name="pick_pieces",
    )(index, *blocks)


def take_rows(value, index):
    return value.at[index].get(mode="promise_in_bounds")


def body(
    tokens, route_ids, route_weights, train_map, serve_place, train_gate, train_up, train_down
):
    plane = lax.axis_index("z")
    line = lax.axis_index(XC)
    quarter = lax.axis_index("y")
    slot_count = serve_place.shape[0]
    part_count = slot_count // EXPERTS
    piece_rows = train_gate.shape[1]
    width = train_gate.shape[2]
    block_rows = piece_rows // PLANE
    steps, tok_count, model_width = tokens.shape
    out_width = model_width // Y
    own_tokens = steps * tok_count
    line_tokens = own_tokens * Z
    capacity = Z * steps * MOST // 2

    slot_iota = jnp.arange(slot_count, dtype=jnp.int32)
    inverse = jnp.sum(
        jnp.where(train_map[:, None] == slot_iota[None, :], slot_iota[:, None], 0), axis=0
    )
    relative = (inverse - plane * PLANE + slot_count) % slot_count
    place_rank = jnp.sum(
        (serve_place[:, None] == serve_place[None, :])
        & (slot_iota[None, :] < slot_iota[:, None]),
        axis=1,
    )
    near_experts = lax.dynamic_slice(serve_place, (plane * PLANE,), (PLANE,))
    near_rank = lax.dynamic_slice(place_rank, (plane * PLANE,), (PLANE,))
    near_count = jnp.sum(near_experts[:, None] == serve_place[None, :], axis=1)
    wanted = near_experts[:, None] * part_count + jnp.arange(part_count, dtype=jnp.int32)[None, :]
    chosen = take_rows(relative // PLANE * 16 + relative % PLANE, wanted)
    chosen_slot = take_rows(inverse, wanted)

    def spread(piece):
        return exchange(piece.reshape(PLANE, block_rows, width), XC)

    def gather_planes(block):
        rows = lax.all_gather(block.reshape(-1, width), "z", axis=0, tiled=True)
        return rows.reshape(slot_count, block_rows, width)

    def assemble(arrived):
        return jnp.swapaxes(arrived, 0, 1).reshape(1, part_count * piece_rows, width)

    experts = jnp.arange(EXPERTS, dtype=jnp.int32)
    hot = route_ids.reshape(own_tokens, -1)[:, :, None] == experts
    named = jnp.any(hot, axis=1).astype(jnp.bfloat16)
    weight = jnp.sum(
        jnp.where(hot, route_weights.reshape(own_tokens, -1)[:, :, None], 0.0), axis=1
    )
    high = weight.astype(jnp.bfloat16)
    rest = weight - high.astype(jnp.float32)
    middle = rest.astype(jnp.bfloat16)
    low = (rest - middle.astype(jnp.float32)).astype(jnp.bfloat16)
    own_rows = lax.dynamic_slice(
        tokens.reshape(own_tokens, model_width),
        (0, quarter * out_width),
        (own_tokens, out_width),
    )
    own_block = jnp.concatenate([own_rows, named, high, middle, low], axis=1)
    block_gate = spread(train_gate)
    block_gate, train_up, own_block = lax.optimization_barrier((block_gate, train_up, own_block))
    gate_all = gather_planes(block_gate)
    block_up = spread(train_up)
    block_up, train_down = lax.optimization_barrier((block_up, train_down))
    up_all = gather_planes(block_up)
    own_block = jnp.pad(own_block, ((0, 0), (0, -own_block.shape[1] % 128)))
    token_ring = Ring(own_block.reshape(2, own_tokens // 2, -1)).hop().hop().hop().hop()
    train_down = token_ring.hold(train_down)
    block_down = spread(train_down)
    planes = jnp.arange(Z, dtype=jnp.int32)
    line_block = token_ring.pick(((planes - plane + Z) % Z * 16)[:, None] + jnp.arange(2)[None, :])
    line_block = line_block.reshape(line_tokens, -1)
    line_rows = line_block[:, :out_width]
    line_routes = line_block[:, out_width : out_width + 4 * EXPERTS]
    token_iota = jnp.arange(line_tokens, dtype=jnp.int32)
    earlier = (token_iota[None, :] < token_iota[:, None]).astype(jnp.bfloat16)
    near_hot = near_experts[:, None] == experts[None, :]

    def place(routes, line_index):
        names = routes[..., :EXPERTS]
        seen = jnp.einsum("ut,lte->lue", earlier, names, preferred_element_type=jnp.float32)

        def of_near(table):
            return jnp.sum(
                jnp.where(near_hot[None, :, None, :], table.astype(jnp.float32)[:, None], 0.0), axis=3
            )

        near_seen = of_near(seen).astype(jnp.int32)
        turn = (near_seen + line_index[:, None, None]) % near_count[None, :, None]
        position = near_seen // near_count[None, :, None]
        sent = (of_near(names) > 0.5) & (turn == near_rank[None, :, None])
        rows = jnp.arange(capacity, dtype=jnp.int32)[None, None, :, None]
        return sent[:, :, None, :] & (position[:, :, None, :] == rows)

    own_placing = place(line_routes[None], line[None])[0].astype(jnp.bfloat16)
    send_rows = jnp.einsum(
        "spt,td->spd", own_placing, line_rows, preferred_element_type=jnp.float32
    ).astype(jnp.bfloat16)
    route_rows = line_routes.reshape(-1, out_width)
    send_rows = jnp.concatenate(
        [send_rows, jnp.broadcast_to(route_rows, (PLANE,) + route_rows.shape)], axis=1
    )
    received = exchange(send_rows, XC)
    quarters = received[:, :capacity].reshape(PLANE * capacity, out_width)
    half = quarters.shape[0] // 2
    to_next = [(i, (i + 1) % Y) for i in range(Y)]
    to_last = [(i, (i - 1) % Y) for i in range(Y)]
    from_last = lax.ppermute(quarters, "y", to_next)
    from_next = lax.ppermute(quarters, "y", to_last)
    gate_all, from_last, from_next = lax.optimization_barrier((gate_all, from_last, from_next))
    far = [
        lax.ppermute(from_last[:half], "y", to_next),
        lax.ppermute(from_next[half:], "y", to_last),
    ]
    inputs = take_rows(
        jnp.stack([quarters, from_next, jnp.concatenate(far, axis=0), from_last]),
        (jnp.arange(Y, dtype=jnp.int32) - quarter + Y) % Y,
    )
    up_all, inputs, block_down = lax.optimization_barrier((up_all, inputs, block_down))
    routes = received[:, capacity:].reshape(PLANE, line_tokens, -1)
    placing = place(routes, jnp.arange(PLANE, dtype=jnp.int32))
    weights = sum(
        routes[..., k * EXPERTS : (k + 1) * EXPERTS].astype(jnp.float32) for k in (1, 2, 3)
    )
    own_expert = lax.dynamic_slice(near_experts, (line,), (1,))
    own_weight = jnp.sum(jnp.where(experts == own_expert, weights, 0.0), axis=2)
    own_sent = lax.dynamic_slice(
        placing, (0, line, 0, 0), (PLANE, 1, capacity, line_tokens)
    )[:, 0]
    row_weight = jnp.sum(jnp.where(own_sent, own_weight[:, None, :], 0.0), axis=2)
    placing = placing.astype(jnp.bfloat16)

    by_part = (part_count, piece_rows, width)
    serve_gate = assemble(exchange(take_rows(gate_all, chosen_slot), XC))
    arrived_up = exchange(take_rows(up_all, chosen_slot), XC)
    gate_act = jnp.einsum(
        "ymd,ydf->mf", inputs, serve_gate.reshape(by_part), preferred_element_type=jnp.float32
    )
    arrived_up, gate_act = lax.optimization_barrier((arrived_up, gate_act))
    down_ring = Ring(block_down).hop()
    arrived_up = down_ring.hold(arrived_up)
    down_ring.hop()
    serve_up = assemble(arrived_up)
    up_act = jnp.einsum(
        "ymd,ydf->mf", inputs, serve_up.reshape(by_part), preferred_element_type=jnp.float32
    )
    hidden = (jax.nn.silu(gate_act) * up_act * row_weight.reshape(-1, 1)).astype(jnp.bfloat16)

    hidden = down_ring.hold(hidden)
    down_ring.hop().hop()

    plane_hidden = lax.all_gather(hidden, XC, axis=0, tiled=False).reshape(
        PLANE, PLANE, capacity, width
    )
    down_rows = down_ring.pick(chosen).reshape(PLANE, part_count, block_rows, width)
    serve_down = assemble(exchange(down_rows, XC))
    partial_value = jnp.einsum(
        "slpf,syrf->slpyr", plane_hidden, down_rows, preferred_element_type=jnp.float32
    ).astype(jnp.bfloat16)
    plane_out = jnp.einsum(
        "lspt,slpyr->yltr", placing, partial_value, preferred_element_type=jnp.float32
    ).astype(jnp.bfloat16)
    line_out = lax.psum_scatter(
        plane_out.reshape(-1, block_rows), "y", scatter_dimension=0, tiled=True
    )
    home = exchange(
        jnp.swapaxes(line_out.reshape(PLANE, Z, own_tokens, block_rows), 0, 1).reshape(
            Z * PLANE, own_tokens, block_rows
        ),
        EP,
    )
    total = jnp.sum(
        home.reshape(Z, PLANE, own_tokens, block_rows).astype(jnp.float32), axis=0
    ).astype(jnp.bfloat16)
    moe_out = jnp.swapaxes(total, 0, 1).reshape(steps, tok_count, out_width)
    return (serve_gate, serve_up, serve_down, moe_out)


def solution(mesh):
    fine = Mesh(mesh.devices.reshape(Z, X, C, Y), ("z", "x", "c", "y"))
    in_specs = (
        P(None, EP, None),
        P(None, EP, None),
        P(None, EP, None),
        P(),
        P(),
        P(EP, None, "y"),
        P(EP, None, "y"),
        P(EP, None, "y"),
    )
    out_specs = (P(EP, None, "y"), P(EP, None, "y"), P(EP, None, "y"), P(None, EP, "y"))
    return jax.shard_map(body, mesh=fine, in_specs=in_specs, out_specs=out_specs, check_vma=False)
```

```python
import jax
import jax.numpy as jnp
from jax import lax
from jax.experimental import pallas as pl
from jax.experimental.pallas import tpu as pltpu
from jax.sharding import Mesh, PartitionSpec as P

EXPERTS = 16
MOST = 10
Z, X, C, Y = 8, 4, 2, 4
PLANE = X * C
EP = ("z", "x", "c")
XC = ("x", "c")


def exchange(value, axes):
    return lax.all_to_all(value, axes, split_axis=0, concat_axis=0, tiled=True)


def shift(value, step):
    return lax.ppermute(value, "z", [(i, (i + step) % Z) for i in range(Z)])


class Ring:
    def __init__(self, block):
        self.ahead = [block]
        self.behind = [block]
        self.far = []

    def hop(self):
        if len(self.ahead) < Z // 2:
            self.behind.append(shift(self.behind[-1], 1))
            self.ahead.append(shift(self.ahead[-1], -1))
        else:
            half = self.ahead[0].shape[0] // 2
            self.far = [shift(self.behind[-1][:half], 1), shift(self.ahead[-1][half:], -1)]
        return self

    def hold(self, value):
        last = self.far or [self.behind[-1], self.ahead[-1]]
        value, held = lax.optimization_barrier((value, last))
        if self.far:
            self.far = held
        else:
            self.behind[-1], self.ahead[-1] = held
        return value

    def pick(self, index):
        blocks = self.ahead + self.far + self.behind[:0:-1]
        return pick_pieces(index.reshape(-1), blocks)


def pick_kernel(index_ref, *refs):
    blocks, out_ref, held_ref, read_sems, write_sems = refs[:-4], *refs[-4:]
    count = out_ref.shape[0]
    half = blocks[Z // 2].shape[0]

    def read(i, carry):
        distance = index_ref[i] >> 4
        place = index_ref[i] & 15

        def copy(block, piece):
            pltpu.make_async_copy(block.at[piece], held_ref.at[i], read_sems.at[i]).start()

        for k in range(Z):
            if k == Z // 2:
                pl.when((distance == k) & (place < half))(lambda: copy(blocks[Z // 2], place))
                pl.when((distance == k) & (place >= half))(
                    lambda: copy(blocks[Z // 2 + 1], place - half)
                )
            else:
                block = blocks[k if k < Z // 2 else k + 1]
                pl.when(distance == k)(lambda block=block: copy(block, place))
        return carry

    def write(i, carry):
        pltpu.make_async_copy(blocks[0].at[0], held_ref.at[i], read_sems.at[i]).wait()
        pltpu.make_async_copy(held_ref.at[i], out_ref.at[i], write_sems.at[i]).start()
        return carry

    def finish(i, carry):
        pltpu.make_async_copy(held_ref.at[i], out_ref.at[i], write_sems.at[i]).wait()
        return carry

    lax.fori_loop(0, count, read, 0)
    lax.fori_loop(0, count, write, 0)
    lax.fori_loop(0, count, finish, 0)


def pick_pieces(index, blocks):
    count = index.shape[0]
    shape = (count,) + blocks[0].shape[1:]
    return pl.pallas_call(
        pick_kernel,
        out_shape=jax.ShapeDtypeStruct(shape, blocks[0].dtype),
        in_specs=[pl.BlockSpec(memory_space=pltpu.SMEM)]
        + [pl.BlockSpec(memory_space=pl.ANY)] * len(blocks),
        out_specs=pl.BlockSpec(memory_space=pl.ANY),
        scratch_shapes=[
            pltpu.VMEM(shape, blocks[0].dtype),
            pltpu.SemaphoreType.DMA((count,)),
            pltpu.SemaphoreType.DMA((count,)),
        ],
        name="pick_pieces",
    )(index, *blocks)


def take_rows(value, index):
    return value.at[index].get(mode="promise_in_bounds")


def body(
    tokens, route_ids, route_weights, train_map, serve_place, train_gate, train_up, train_down
):
    plane = lax.axis_index("z")
    line = lax.axis_index(XC)
    quarter = lax.axis_index("y")
    slot_count = serve_place.shape[0]
    part_count = slot_count // EXPERTS
    piece_rows = train_gate.shape[1]
    width = train_gate.shape[2]
    block_rows = piece_rows // PLANE
    steps, tok_count, model_width = tokens.shape
    out_width = model_width // Y
    own_tokens = steps * tok_count
    line_tokens = own_tokens * Z
    capacity = Z * steps * MOST // 2

    slot_iota = jnp.arange(slot_count, dtype=jnp.int32)
    inverse = jnp.sum(
        jnp.where(train_map[:, None] == slot_iota[None, :], slot_iota[:, None], 0), axis=0
    )
    relative = (inverse - plane * PLANE + slot_count) % slot_count
    place_rank = jnp.sum(
        (serve_place[:, None] == serve_place[None, :])
        & (slot_iota[None, :] < slot_iota[:, None]),
        axis=1,
    )
    near_experts = lax.dynamic_slice(serve_place, (plane * PLANE,), (PLANE,))
    near_rank = lax.dynamic_slice(place_rank, (plane * PLANE,), (PLANE,))
    near_count = jnp.sum(near_experts[:, None] == serve_place[None, :], axis=1)
    wanted = near_experts[:, None] * part_count + jnp.arange(part_count, dtype=jnp.int32)[None, :]
    chosen = take_rows(relative // PLANE * 16 + relative % PLANE, wanted)
    chosen_slot = take_rows(inverse, wanted)

    def spread(piece):
        return exchange(piece.reshape(PLANE, block_rows, width), XC)

    def gather_planes(block):
        rows = lax.all_gather(block.reshape(-1, width), "z", axis=0, tiled=True)
        return rows.reshape(slot_count, block_rows, width)

    def assemble(arrived):
        return jnp.swapaxes(arrived, 0, 1).reshape(1, part_count * piece_rows, width)

    experts = jnp.arange(EXPERTS, dtype=jnp.int32)
    hot = route_ids.reshape(own_tokens, -1)[:, :, None] == experts
    named = jnp.any(hot, axis=1).astype(jnp.bfloat16)
    weight = jnp.sum(
        jnp.where(hot, route_weights.reshape(own_tokens, -1)[:, :, None], 0.0), axis=1
    )
    high = weight.astype(jnp.bfloat16)
    rest = weight - high.astype(jnp.float32)
    middle = rest.astype(jnp.bfloat16)
    low = (rest - middle.astype(jnp.float32)).astype(jnp.bfloat16)
    own_rows = lax.dynamic_slice(
        tokens.reshape(own_tokens, model_width),
        (0, quarter * out_width),
        (own_tokens, out_width),
    )
    own_block = jnp.concatenate([own_rows, named, high, middle, low], axis=1)
    block_gate = spread(train_gate)
    block_gate, train_up, own_block = lax.optimization_barrier((block_gate, train_up, own_block))
    gate_all = gather_planes(block_gate)
    block_up = spread(train_up)
    block_up, train_down = lax.optimization_barrier((block_up, train_down))
    up_all = gather_planes(block_up)
    own_block = jnp.pad(own_block, ((0, 0), (0, -own_block.shape[1] % 128)))
    token_ring = Ring(own_block.reshape(2, own_tokens // 2, -1)).hop().hop().hop().hop()
    train_down = token_ring.hold(train_down)
    block_down = spread(train_down)
    planes = jnp.arange(Z, dtype=jnp.int32)
    line_block = token_ring.pick(((planes - plane + Z) % Z * 16)[:, None] + jnp.arange(2)[None, :])
    line_block = line_block.reshape(line_tokens, -1)
    line_rows = line_block[:, :out_width]
    line_routes = line_block[:, out_width : out_width + 4 * EXPERTS]
    token_iota = jnp.arange(line_tokens, dtype=jnp.int32)
    earlier = (token_iota[None, :] < token_iota[:, None]).astype(jnp.bfloat16)
    near_hot = near_experts[:, None] == experts[None, :]

    def place(routes, line_index):
        names = routes[..., :EXPERTS]
        seen = jnp.einsum("ut,lte->lue", earlier, names, preferred_element_type=jnp.float32)

        def of_near(table):
            return jnp.sum(
                jnp.where(near_hot[None, :, None, :], table.astype(jnp.float32)[:, None], 0.0), axis=3
            )

        near_seen = of_near(seen).astype(jnp.int32)
        turn = (near_seen + line_index[:, None, None]) % near_count[None, :, None]
        position = near_seen // near_count[None, :, None]
        sent = (of_near(names) > 0.5) & (turn == near_rank[None, :, None])
        rows = jnp.arange(capacity, dtype=jnp.int32)[None, None, :, None]
        return sent[:, :, None, :] & (position[:, :, None, :] == rows)

    own_placing = place(line_routes[None], line[None])[0].astype(jnp.bfloat16)
    send_rows = jnp.einsum(
        "spt,td->spd", own_placing, line_rows, preferred_element_type=jnp.float32
    ).astype(jnp.bfloat16)
    route_rows = line_routes.reshape(-1, out_width)
    send_rows = jnp.concatenate(
        [send_rows, jnp.broadcast_to(route_rows, (PLANE,) + route_rows.shape)], axis=1
    )
    received = exchange(send_rows, XC)
    quarters = received[:, :capacity].reshape(PLANE * capacity, out_width)
    half = quarters.shape[0] // 2
    to_next = [(i, (i + 1) % Y) for i in range(Y)]
    to_last = [(i, (i - 1) % Y) for i in range(Y)]
    from_last = lax.ppermute(quarters, "y", to_next)
    from_next = lax.ppermute(quarters, "y", to_last)
    gate_all, from_last, from_next = lax.optimization_barrier((gate_all, from_last, from_next))
    far = [
        lax.ppermute(from_last[:half], "y", to_next),
        lax.ppermute(from_next[half:], "y", to_last),
    ]
    far, block_down = lax.optimization_barrier((far, block_down))
    inputs = take_rows(
        jnp.stack([quarters, from_next, jnp.concatenate(far, axis=0), from_last]),
        (jnp.arange(Y, dtype=jnp.int32) - quarter + Y) % Y,
    )
    up_all, inputs = lax.optimization_barrier((up_all, inputs))
    routes = received[:, capacity:].reshape(PLANE, line_tokens, -1)
    placing = place(routes, jnp.arange(PLANE, dtype=jnp.int32))
    weights = sum(
        routes[..., k * EXPERTS : (k + 1) * EXPERTS].astype(jnp.float32) for k in (1, 2, 3)
    )
    own_expert = lax.dynamic_slice(near_experts, (line,), (1,))
    own_weight = jnp.sum(jnp.where(experts == own_expert, weights, 0.0), axis=2)
    own_sent = lax.dynamic_slice(
        placing, (0, line, 0, 0), (PLANE, 1, capacity, line_tokens)
    )[:, 0]
    row_weight = jnp.sum(jnp.where(own_sent, own_weight[:, None, :], 0.0), axis=2)
    placing = placing.astype(jnp.bfloat16)

    by_part = (part_count, piece_rows, width)
    serve_gate = assemble(exchange(take_rows(gate_all, chosen_slot), XC))
    arrived_up = exchange(take_rows(up_all, chosen_slot), XC)
    down_ring = Ring(block_down).hop()
    inputs = down_ring.hold(inputs)
    gate_act = jnp.einsum(
        "ymd,ydf->mf", inputs, serve_gate.reshape(by_part), preferred_element_type=jnp.float32
    )
    arrived_up, gate_act = lax.optimization_barrier((arrived_up, gate_act))
    down_ring.hop()
    arrived_up = down_ring.hold(arrived_up)
    down_ring.hop()
    serve_up = assemble(arrived_up)
    up_act = jnp.einsum(
        "ymd,ydf->mf", inputs, serve_up.reshape(by_part), preferred_element_type=jnp.float32
    )
    hidden = (jax.nn.silu(gate_act) * up_act * row_weight.reshape(-1, 1)).astype(jnp.bfloat16)

    down_ring.hop()

    plane_hidden = lax.all_gather(hidden, XC, axis=0, tiled=False).reshape(
        PLANE, PLANE, capacity, width
    )
    down_rows = down_ring.pick(chosen).reshape(PLANE, part_count, block_rows, width)
    serve_down = assemble(exchange(down_rows, XC))
    partial_value = jnp.einsum(
        "slpf,syrf->slpyr", plane_hidden, down_rows, preferred_element_type=jnp.float32
    ).astype(jnp.bfloat16)
    plane_out = jnp.einsum(
        "lspt,slpyr->yltr", placing, partial_value, preferred_element_type=jnp.float32
    ).astype(jnp.bfloat16)
    line_out = lax.psum_scatter(
        plane_out.reshape(-1, block_rows), "y", scatter_dimension=0, tiled=True
    )
    home = exchange(
        jnp.swapaxes(line_out.reshape(PLANE, Z, own_tokens, block_rows), 0, 1).reshape(
            Z * PLANE, own_tokens, block_rows
        ),
        EP,
    )
    total = jnp.sum(
        home.reshape(Z, PLANE, own_tokens, block_rows).astype(jnp.float32), axis=0
    ).astype(jnp.bfloat16)
    moe_out = jnp.swapaxes(total, 0, 1).reshape(steps, tok_count, out_width)
    return (serve_gate, serve_up, serve_down, moe_out)


def solution(mesh):
    fine = Mesh(mesh.devices.reshape(Z, X, C, Y), ("z", "x", "c", "y"))
    in_specs = (
        P(None, EP, None),
        P(None, EP, None),
        P(None, EP, None),
        P(),
        P(),
        P(EP, None, "y"),
        P(EP, None, "y"),
        P(EP, None, "y"),
    )
    out_specs = (P(EP, None, "y"), P(EP, None, "y"), P(EP, None, "y"), P(None, EP, "y"))
    return jax.shard_map(body, mesh=fine, in_specs=in_specs, out_specs=out_specs, check_vma=False)
```

```python
import jax
import jax.numpy as jnp
from jax import lax
from jax.experimental import pallas as pl
from jax.experimental.pallas import tpu as pltpu
from jax.sharding import Mesh, PartitionSpec as P

EXPERTS = 16
MOST = 10
Z, X, C, Y = 8, 4, 2, 4
PLANE = X * C
EP = ("z", "x", "c")
XC = ("x", "c")


def exchange(value, axes):
    return lax.all_to_all(value, axes, split_axis=0, concat_axis=0, tiled=True)


def shift(value, step):
    return lax.ppermute(value, "z", [(i, (i + step) % Z) for i in range(Z)])


class Ring:
    def __init__(self, block):
        self.ahead = [block]
        self.behind = [block]
        self.far = []

    def hop(self):
        if len(self.ahead) < Z // 2:
            self.behind.append(shift(self.behind[-1], 1))
            self.ahead.append(shift(self.ahead[-1], -1))
        else:
            half = self.ahead[0].shape[0] // 2
            self.far = [shift(self.behind[-1][:half], 1), shift(self.ahead[-1][half:], -1)]
        return self

    def hold(self, value):
        last = self.far or [self.behind[-1], self.ahead[-1]]
        value, held = lax.optimization_barrier((value, last))
        if self.far:
            self.far = held
        else:
            self.behind[-1], self.ahead[-1] = held
        return value

    def pick(self, index):
        blocks = self.ahead + self.far + self.behind[:0:-1]
        return pick_pieces(index.reshape(-1), blocks)


def pick_kernel(index_ref, *refs):
    blocks, out_ref, held_ref, read_sems, write_sems = refs[:-4], *refs[-4:]
    count = out_ref.shape[0]
    half = blocks[Z // 2].shape[0]

    def read(i, carry):
        distance = index_ref[i] >> 4
        place = index_ref[i] & 15

        def copy(block, piece):
            pltpu.make_async_copy(block.at[piece], held_ref.at[i], read_sems.at[i]).start()

        for k in range(Z):
            if k == Z // 2:
                pl.when((distance == k) & (place < half))(lambda: copy(blocks[Z // 2], place))
                pl.when((distance == k) & (place >= half))(
                    lambda: copy(blocks[Z // 2 + 1], place - half)
                )
            else:
                block = blocks[k if k < Z // 2 else k + 1]
                pl.when(distance == k)(lambda block=block: copy(block, place))
        return carry

    def write(i, carry):
        pltpu.make_async_copy(blocks[0].at[0], held_ref.at[i], read_sems.at[i]).wait()
        pltpu.make_async_copy(held_ref.at[i], out_ref.at[i], write_sems.at[i]).start()
        return carry

    def finish(i, carry):
        pltpu.make_async_copy(held_ref.at[i], out_ref.at[i], write_sems.at[i]).wait()
        return carry

    lax.fori_loop(0, count, read, 0)
    lax.fori_loop(0, count, write, 0)
    lax.fori_loop(0, count, finish, 0)


def pick_pieces(index, blocks):
    count = index.shape[0]
    shape = (count,) + blocks[0].shape[1:]
    return pl.pallas_call(
        pick_kernel,
        out_shape=jax.ShapeDtypeStruct(shape, blocks[0].dtype),
        in_specs=[pl.BlockSpec(memory_space=pltpu.SMEM)]
        + [pl.BlockSpec(memory_space=pl.ANY)] * len(blocks),
        out_specs=pl.BlockSpec(memory_space=pl.ANY),
        scratch_shapes=[
            pltpu.VMEM(shape, blocks[0].dtype),
            pltpu.SemaphoreType.DMA((count,)),
            pltpu.SemaphoreType.DMA((count,)),
        ],
        name="pick_pieces",
    )(index, *blocks)


def take_rows(value, index):
    return value.at[index].get(mode="promise_in_bounds")


def body(
    tokens, route_ids, route_weights, train_map, serve_place, train_gate, train_up, train_down
):
    plane = lax.axis_index("z")
    line = lax.axis_index(XC)
    quarter = lax.axis_index("y")
    slot_count = serve_place.shape[0]
    part_count = slot_count // EXPERTS
    piece_rows = train_gate.shape[1]
    width = train_gate.shape[2]
    block_rows = piece_rows // PLANE
    steps, tok_count, model_width = tokens.shape
    out_width = model_width // Y
    own_tokens = steps * tok_count
    line_tokens = own_tokens * Z
    capacity = Z * steps * MOST // 2

    slot_iota = jnp.arange(slot_count, dtype=jnp.int32)
    inverse = jnp.sum(
        jnp.where(train_map[:, None] == slot_iota[None, :], slot_iota[:, None], 0), axis=0
    )
    relative = (inverse - plane * PLANE + slot_count) % slot_count
    place_rank = jnp.sum(
        (serve_place[:, None] == serve_place[None, :])
        & (slot_iota[None, :] < slot_iota[:, None]),
        axis=1,
    )
    near_experts = lax.dynamic_slice(serve_place, (plane * PLANE,), (PLANE,))
    near_rank = lax.dynamic_slice(place_rank, (plane * PLANE,), (PLANE,))
    near_count = jnp.sum(near_experts[:, None] == serve_place[None, :], axis=1)
    wanted = near_experts[:, None] * part_count + jnp.arange(part_count, dtype=jnp.int32)[None, :]
    chosen = take_rows(relative // PLANE * 16 + relative % PLANE, wanted)
    chosen_slot = take_rows(inverse, wanted)

    def spread(piece):
        return exchange(piece.reshape(PLANE, block_rows, width), XC)

    def gather_planes(block):
        rows = lax.all_gather(block.reshape(-1, width), "z", axis=0, tiled=True)
        return rows.reshape(slot_count, block_rows, width)

    def assemble(arrived):
        return jnp.swapaxes(arrived, 0, 1).reshape(1, part_count * piece_rows, width)

    experts = jnp.arange(EXPERTS, dtype=jnp.int32)
    hot = route_ids.reshape(own_tokens, -1)[:, :, None] == experts
    named = jnp.any(hot, axis=1).astype(jnp.bfloat16)
    weight = jnp.sum(
        jnp.where(hot, route_weights.reshape(own_tokens, -1)[:, :, None], 0.0), axis=1
    )
    high = weight.astype(jnp.bfloat16)
    rest = weight - high.astype(jnp.float32)
    middle = rest.astype(jnp.bfloat16)
    low = (rest - middle.astype(jnp.float32)).astype(jnp.bfloat16)
    own_rows = lax.dynamic_slice(
        tokens.reshape(own_tokens, model_width),
        (0, quarter * out_width),
        (own_tokens, out_width),
    )
    own_block = jnp.concatenate([own_rows, named, high, middle, low], axis=1)
    block_gate = spread(train_gate)
    block_gate, train_up, own_block = lax.optimization_barrier((block_gate, train_up, own_block))
    gate_all = gather_planes(block_gate)
    block_up = spread(train_up)
    block_up, train_down = lax.optimization_barrier((block_up, train_down))
    up_all = gather_planes(block_up)
    own_block = jnp.pad(own_block, ((0, 0), (0, -own_block.shape[1] % 128)))
    token_ring = Ring(own_block.reshape(2, own_tokens // 2, -1)).hop().hop().hop().hop()
    train_down = token_ring.hold(train_down)
    block_down = spread(train_down)
    planes = jnp.arange(Z, dtype=jnp.int32)
    line_block = token_ring.pick(((planes - plane + Z) % Z * 16)[:, None] + jnp.arange(2)[None, :])
    line_block = line_block.reshape(line_tokens, -1)
    line_rows = line_block[:, :out_width]
    line_routes = line_block[:, out_width : out_width + 4 * EXPERTS]
    token_iota = jnp.arange(line_tokens, dtype=jnp.int32)
    earlier = (token_iota[None, :] < token_iota[:, None]).astype(jnp.bfloat16)
    near_hot = near_experts[:, None] == experts[None, :]

    def place(routes, line_index):
        names = routes[..., :EXPERTS]
        seen = jnp.einsum("ut,lte->lue", earlier, names, preferred_element_type=jnp.float32)

        def of_near(table):
            return jnp.sum(
                jnp.where(near_hot[None, :, None, :], table.astype(jnp.float32)[:, None], 0.0), axis=3
            )

        near_seen = of_near(seen).astype(jnp.int32)
        turn = (near_seen + line_index[:, None, None]) % near_count[None, :, None]
        position = near_seen // near_count[None, :, None]
        sent = (of_near(names) > 0.5) & (turn == near_rank[None, :, None])
        rows = jnp.arange(capacity, dtype=jnp.int32)[None, None, :, None]
        return sent[:, :, None, :] & (position[:, :, None, :] == rows)

    own_placing = place(line_routes[None], line[None])[0].astype(jnp.bfloat16)
    send_rows = jnp.einsum(
        "spt,td->spd", own_placing, line_rows, preferred_element_type=jnp.float32
    ).astype(jnp.bfloat16)
    route_rows = line_routes.reshape(-1, out_width)
    send_rows = jnp.concatenate(
        [send_rows, jnp.broadcast_to(route_rows, (PLANE,) + route_rows.shape)], axis=1
    )
    received = exchange(send_rows, XC)
    quarters = received[:, :capacity].reshape(PLANE * capacity, out_width)
    half = quarters.shape[0] // 2
    to_next = [(i, (i + 1) % Y) for i in range(Y)]
    to_last = [(i, (i - 1) % Y) for i in range(Y)]
    from_last = lax.ppermute(quarters, "y", to_next)
    from_next = lax.ppermute(quarters, "y", to_last)
    gate_all, block_down, from_last, from_next = lax.optimization_barrier(
        (gate_all, block_down, from_last, from_next)
    )
    far = [
        lax.ppermute(from_last[:half], "y", to_next),
        lax.ppermute(from_next[half:], "y", to_last),
    ]
    down_all = gather_planes(block_down)
    inputs = take_rows(
        jnp.stack([quarters, from_next, jnp.concatenate(far, axis=0), from_last]),
        (jnp.arange(Y, dtype=jnp.int32) - quarter + Y) % Y,
    )
    up_all, inputs = lax.optimization_barrier((up_all, inputs))
    routes = received[:, capacity:].reshape(PLANE, line_tokens, -1)
    placing = place(routes, jnp.arange(PLANE, dtype=jnp.int32))
    weights = sum(
        routes[..., k * EXPERTS : (k + 1) * EXPERTS].astype(jnp.float32) for k in (1, 2, 3)
    )
    own_expert = lax.dynamic_slice(near_experts, (line,), (1,))
    own_weight = jnp.sum(jnp.where(experts == own_expert, weights, 0.0), axis=2)
    own_sent = lax.dynamic_slice(
        placing, (0, line, 0, 0), (PLANE, 1, capacity, line_tokens)
    )[:, 0]
    row_weight = jnp.sum(jnp.where(own_sent, own_weight[:, None, :], 0.0), axis=2)
    placing = placing.astype(jnp.bfloat16)

    by_part = (part_count, piece_rows, width)
    serve_gate = assemble(exchange(take_rows(gate_all, chosen_slot), XC))
    arrived_up = exchange(take_rows(up_all, chosen_slot), XC)
    gate_act = jnp.einsum(
        "ymd,ydf->mf", inputs, serve_gate.reshape(by_part), preferred_element_type=jnp.float32
    )
    arrived_up, gate_act = lax.optimization_barrier((arrived_up, gate_act))
    serve_up = assemble(arrived_up)
    up_act = jnp.einsum(
        "ymd,ydf->mf", inputs, serve_up.reshape(by_part), preferred_element_type=jnp.float32
    )
    hidden = (jax.nn.silu(gate_act) * up_act * row_weight.reshape(-1, 1)).astype(jnp.bfloat16)


    plane_hidden = lax.all_gather(hidden, XC, axis=0, tiled=False).reshape(
        PLANE, PLANE, capacity, width
    )
    down_rows = take_rows(down_all, chosen_slot)
    half_parts = part_count // 2
    arrived_down = [exchange(down_rows[:, :half_parts], XC), exchange(down_rows[:, half_parts:], XC)]
    down_rows, arrived_down[0] = lax.optimization_barrier((down_rows, arrived_down[0]))
    serve_down = assemble(jnp.concatenate(arrived_down, axis=1))
    partial_value = jnp.einsum(
        "slpf,syrf->slpyr", plane_hidden, down_rows, preferred_element_type=jnp.float32
    ).astype(jnp.bfloat16)
    plane_out = jnp.einsum(
        "lspt,slpyr->yltr", placing, partial_value, preferred_element_type=jnp.float32
    ).astype(jnp.bfloat16)
    line_out = lax.psum_scatter(
        plane_out.reshape(-1, block_rows), "y", scatter_dimension=0, tiled=True
    )
    home = exchange(
        jnp.swapaxes(line_out.reshape(PLANE, Z, own_tokens, block_rows), 0, 1).reshape(
            Z * PLANE, own_tokens, block_rows
        ),
        EP,
    )
    total = jnp.sum(
        home.reshape(Z, PLANE, own_tokens, block_rows).astype(jnp.float32), axis=0
    ).astype(jnp.bfloat16)
    moe_out = jnp.swapaxes(total, 0, 1).reshape(steps, tok_count, out_width)
    return (serve_gate, serve_up, serve_down, moe_out)


def solution(mesh):
    fine = Mesh(mesh.devices.reshape(Z, X, C, Y), ("z", "x", "c", "y"))
    in_specs = (
        P(None, EP, None),
        P(None, EP, None),
        P(None, EP, None),
        P(),
        P(),
        P(EP, None, "y"),
        P(EP, None, "y"),
        P(EP, None, "y"),
    )
    out_specs = (P(EP, None, "y"), P(EP, None, "y"), P(EP, None, "y"), P(None, EP, "y"))
    return jax.shard_map(body, mesh=fine, in_specs=in_specs, out_specs=out_specs, check_vma=False)
```

```python
import jax
import jax.numpy as jnp
from jax import lax
from jax.experimental import pallas as pl
from jax.experimental.pallas import tpu as pltpu
from jax.sharding import Mesh, PartitionSpec as P

EXPERTS = 16
MOST = 10
Z, X, C, Y = 8, 4, 2, 4
PLANE = X * C
EP = ("z", "x", "c")
XC = ("x", "c")


def exchange(value, axes):
    return lax.all_to_all(value, axes, split_axis=0, concat_axis=0, tiled=True)


def shift(value, step):
    return lax.ppermute(value, "z", [(i, (i + step) % Z) for i in range(Z)])


class Ring:
    def __init__(self, block):
        self.ahead = [block]
        self.behind = [block]
        self.far = []

    def hop(self):
        if len(self.ahead) < Z // 2:
            self.behind.append(shift(self.behind[-1], 1))
            self.ahead.append(shift(self.ahead[-1], -1))
        else:
            half = self.ahead[0].shape[0] // 2
            self.far = [shift(self.behind[-1][:half], 1), shift(self.ahead[-1][half:], -1)]
        return self

    def hold(self, value):
        last = self.far or [self.behind[-1], self.ahead[-1]]
        value, held = lax.optimization_barrier((value, last))
        if self.far:
            self.far = held
        else:
            self.behind[-1], self.ahead[-1] = held
        return value

    def pick(self, index):
        blocks = self.ahead + self.far + self.behind[:0:-1]
        return pick_pieces(index.reshape(-1), blocks)


def pick_kernel(index_ref, *refs):
    blocks, out_ref, held_ref, read_sems, write_sems = refs[:-4], *refs[-4:]
    count = out_ref.shape[0]
    half = blocks[Z // 2].shape[0]

    def read(i, carry):
        distance = index_ref[i] >> 4
        place = index_ref[i] & 15

        def copy(block, piece):
            pltpu.make_async_copy(block.at[piece], held_ref.at[i], read_sems.at[i]).start()

        for k in range(Z):
            if k == Z // 2:
                pl.when((distance == k) & (place < half))(lambda: copy(blocks[Z // 2], place))
                pl.when((distance == k) & (place >= half))(
                    lambda: copy(blocks[Z // 2 + 1], place - half)
                )
            else:
                block = blocks[k if k < Z // 2 else k + 1]
                pl.when(distance == k)(lambda block=block: copy(block, place))
        return carry

    def write(i, carry):
        pltpu.make_async_copy(blocks[0].at[0], held_ref.at[i], read_sems.at[i]).wait()
        pltpu.make_async_copy(held_ref.at[i], out_ref.at[i], write_sems.at[i]).start()
        return carry

    def finish(i, carry):
        pltpu.make_async_copy(held_ref.at[i], out_ref.at[i], write_sems.at[i]).wait()
        return carry

    lax.fori_loop(0, count, read, 0)
    lax.fori_loop(0, count, write, 0)
    lax.fori_loop(0, count, finish, 0)


def pick_pieces(index, blocks):
    count = index.shape[0]
    shape = (count,) + blocks[0].shape[1:]
    return pl.pallas_call(
        pick_kernel,
        out_shape=jax.ShapeDtypeStruct(shape, blocks[0].dtype),
        in_specs=[pl.BlockSpec(memory_space=pltpu.SMEM)]
        + [pl.BlockSpec(memory_space=pl.ANY)] * len(blocks),
        out_specs=pl.BlockSpec(memory_space=pl.ANY),
        scratch_shapes=[
            pltpu.VMEM(shape, blocks[0].dtype),
            pltpu.SemaphoreType.DMA((count,)),
            pltpu.SemaphoreType.DMA((count,)),
        ],
        name="pick_pieces",
    )(index, *blocks)


def take_rows(value, index):
    return value.at[index].get(mode="promise_in_bounds")


def body(
    tokens, route_ids, route_weights, train_map, serve_place, train_gate, train_up, train_down
):
    plane = lax.axis_index("z")
    line = lax.axis_index(XC)
    quarter = lax.axis_index("y")
    slot_count = serve_place.shape[0]
    part_count = slot_count // EXPERTS
    piece_rows = train_gate.shape[1]
    width = train_gate.shape[2]
    block_rows = piece_rows // PLANE
    steps, tok_count, model_width = tokens.shape
    out_width = model_width // Y
    own_tokens = steps * tok_count
    line_tokens = own_tokens * Z
    capacity = Z * steps * MOST // 2

    slot_iota = jnp.arange(slot_count, dtype=jnp.int32)
    inverse = jnp.sum(
        jnp.where(train_map[:, None] == slot_iota[None, :], slot_iota[:, None], 0), axis=0
    )
    relative = (inverse - plane * PLANE + slot_count) % slot_count
    place_rank = jnp.sum(
        (serve_place[:, None] == serve_place[None, :])
        & (slot_iota[None, :] < slot_iota[:, None]),
        axis=1,
    )
    near_experts = lax.dynamic_slice(serve_place, (plane * PLANE,), (PLANE,))
    near_rank = lax.dynamic_slice(place_rank, (plane * PLANE,), (PLANE,))
    near_count = jnp.sum(near_experts[:, None] == serve_place[None, :], axis=1)
    wanted = near_experts[:, None] * part_count + jnp.arange(part_count, dtype=jnp.int32)[None, :]
    chosen = take_rows(relative // PLANE * 16 + relative % PLANE, wanted)
    chosen_slot = take_rows(inverse, wanted)

    def spread(piece):
        return exchange(piece.reshape(PLANE, block_rows, width), XC)

    def gather_planes(block):
        rows = lax.all_gather(block.reshape(-1, width), "z", axis=0, tiled=True)
        return rows.reshape(slot_count, block_rows, width)

    def assemble(arrived):
        return jnp.swapaxes(arrived, 0, 1).reshape(1, part_count * piece_rows, width)

    experts = jnp.arange(EXPERTS, dtype=jnp.int32)
    hot = route_ids.reshape(own_tokens, -1)[:, :, None] == experts
    named = jnp.any(hot, axis=1).astype(jnp.bfloat16)
    weight = jnp.sum(
        jnp.where(hot, route_weights.reshape(own_tokens, -1)[:, :, None], 0.0), axis=1
    )
    high = weight.astype(jnp.bfloat16)
    rest = weight - high.astype(jnp.float32)
    middle = rest.astype(jnp.bfloat16)
    low = (rest - middle.astype(jnp.float32)).astype(jnp.bfloat16)
    own_rows = lax.dynamic_slice(
        tokens.reshape(own_tokens, model_width),
        (0, quarter * out_width),
        (own_tokens, out_width),
    )
    own_block = jnp.concatenate([own_rows, named, high, middle, low], axis=1)
    block_gate = spread(train_gate)
    block_gate, train_up, own_block = lax.optimization_barrier((block_gate, train_up, own_block))
    gate_all = gather_planes(block_gate)
    block_up = spread(train_up)
    block_up, train_down = lax.optimization_barrier((block_up, train_down))
    up_all = gather_planes(block_up)
    own_block = jnp.pad(own_block, ((0, 0), (0, -own_block.shape[1] % 128)))
    token_ring = Ring(own_block.reshape(2, own_tokens // 2, -1)).hop().hop().hop().hop()
    train_down = token_ring.hold(train_down)
    block_down = spread(train_down)
    planes = jnp.arange(Z, dtype=jnp.int32)
    line_block = token_ring.pick(((planes - plane + Z) % Z * 16)[:, None] + jnp.arange(2)[None, :])
    line_block = line_block.reshape(line_tokens, -1)
    line_rows = line_block[:, :out_width]
    line_routes = line_block[:, out_width : out_width + 4 * EXPERTS]
    token_iota = jnp.arange(line_tokens, dtype=jnp.int32)
    earlier = (token_iota[None, :] < token_iota[:, None]).astype(jnp.bfloat16)
    near_hot = near_experts[:, None] == experts[None, :]

    def place(routes, line_index):
        names = routes[..., :EXPERTS]
        seen = jnp.einsum("ut,lte->lue", earlier, names, preferred_element_type=jnp.float32)

        def of_near(table):
            return jnp.sum(
                jnp.where(near_hot[None, :, None, :], table.astype(jnp.float32)[:, None], 0.0), axis=3
            )

        near_seen = of_near(seen).astype(jnp.int32)
        turn = (near_seen + line_index[:, None, None]) % near_count[None, :, None]
        position = near_seen // near_count[None, :, None]
        sent = (of_near(names) > 0.5) & (turn == near_rank[None, :, None])
        rows = jnp.arange(capacity, dtype=jnp.int32)[None, None, :, None]
        return sent[:, :, None, :] & (position[:, :, None, :] == rows)

    own_placing = place(line_routes[None], line[None])[0].astype(jnp.bfloat16)
    send_rows = jnp.einsum(
        "spt,td->spd", own_placing, line_rows, preferred_element_type=jnp.float32
    ).astype(jnp.bfloat16)
    route_rows = line_routes.reshape(-1, out_width)
    send_rows = jnp.concatenate(
        [send_rows, jnp.broadcast_to(route_rows, (PLANE,) + route_rows.shape)], axis=1
    )
    received = exchange(send_rows, XC)
    quarters = received[:, :capacity].reshape(PLANE * capacity, out_width)
    half = quarters.shape[0] // 2
    to_next = [(i, (i + 1) % Y) for i in range(Y)]
    to_last = [(i, (i - 1) % Y) for i in range(Y)]
    from_last = lax.ppermute(quarters, "y", to_next)
    from_next = lax.ppermute(quarters, "y", to_last)
    gate_all, from_last, from_next = lax.optimization_barrier((gate_all, from_last, from_next))
    far = [
        lax.ppermute(from_last[:half], "y", to_next),
        lax.ppermute(from_next[half:], "y", to_last),
    ]
    far, block_down = lax.optimization_barrier((far, block_down))
    inputs = take_rows(
        jnp.stack([quarters, from_next, jnp.concatenate(far, axis=0), from_last]),
        (jnp.arange(Y, dtype=jnp.int32) - quarter + Y) % Y,
    )
    up_all, inputs = lax.optimization_barrier((up_all, inputs))
    routes = received[:, capacity:].reshape(PLANE, line_tokens, -1)
    placing = place(routes, jnp.arange(PLANE, dtype=jnp.int32))
    weights = sum(
        routes[..., k * EXPERTS : (k + 1) * EXPERTS].astype(jnp.float32) for k in (1, 2, 3)
    )
    own_expert = lax.dynamic_slice(near_experts, (line,), (1,))
    own_weight = jnp.sum(jnp.where(experts == own_expert, weights, 0.0), axis=2)
    own_sent = lax.dynamic_slice(
        placing, (0, line, 0, 0), (PLANE, 1, capacity, line_tokens)
    )[:, 0]
    row_weight = jnp.sum(jnp.where(own_sent, own_weight[:, None, :], 0.0), axis=2)
    placing = placing.astype(jnp.bfloat16)

    by_part = (part_count, piece_rows, width)
    serve_gate = assemble(exchange(take_rows(gate_all, chosen_slot), XC))
    arrived_up = exchange(take_rows(up_all, chosen_slot), XC)
    down_ring = Ring(block_down).hop()
    inputs = down_ring.hold(inputs)
    gate_act = jnp.einsum(
        "ymd,ydf->mf", inputs, serve_gate.reshape(by_part), preferred_element_type=jnp.float32
    )
    arrived_up, gate_act = lax.optimization_barrier((arrived_up, gate_act))
    down_ring.hop()
    arrived_up = down_ring.hold(arrived_up)
    down_ring.hop()
    serve_up = assemble(arrived_up)
    up_act = jnp.einsum(
        "ymd,ydf->mf", inputs, serve_up.reshape(by_part), preferred_element_type=jnp.float32
    )
    hidden = (jax.nn.silu(gate_act) * up_act * row_weight.reshape(-1, 1)).astype(jnp.bfloat16)

    down_ring.hop()

    plane_hidden = lax.all_gather(hidden, XC, axis=0, tiled=False).reshape(
        PLANE, PLANE, capacity, width
    )
    down_rows = down_ring.pick(chosen).reshape(PLANE, part_count, block_rows, width)
    early_rows, plane_hidden = lax.optimization_barrier((down_rows[:, :1], plane_hidden))
    arrived_down = [exchange(early_rows, XC), exchange(down_rows[:, 1:], XC)]
    partial_value = jnp.einsum(
        "slpf,syrf->slpyr", plane_hidden, down_rows, preferred_element_type=jnp.float32
    ).astype(jnp.bfloat16)
    plane_out = jnp.einsum(
        "lspt,slpyr->yltr", placing, partial_value, preferred_element_type=jnp.float32
    ).astype(jnp.bfloat16)
    plane_out, arrived_down[0] = lax.optimization_barrier((plane_out, arrived_down[0]))
    serve_down = assemble(jnp.concatenate(arrived_down, axis=1))
    line_out = lax.psum_scatter(
        plane_out.reshape(-1, block_rows), "y", scatter_dimension=0, tiled=True
    )
    home = exchange(
        jnp.swapaxes(line_out.reshape(PLANE, Z, own_tokens, block_rows), 0, 1).reshape(
            Z * PLANE, own_tokens, block_rows
        ),
        EP,
    )
    total = jnp.sum(
        home.reshape(Z, PLANE, own_tokens, block_rows).astype(jnp.float32), axis=0
    ).astype(jnp.bfloat16)
    moe_out = jnp.swapaxes(total, 0, 1).reshape(steps, tok_count, out_width)
    return (serve_gate, serve_up, serve_down, moe_out)


def solution(mesh):
    fine = Mesh(mesh.devices.reshape(Z, X, C, Y), ("z", "x", "c", "y"))
    in_specs = (
        P(None, EP, None),
        P(None, EP, None),
        P(None, EP, None),
        P(),
        P(),
        P(EP, None, "y"),
        P(EP, None, "y"),
        P(EP, None, "y"),
    )
    out_specs = (P(EP, None, "y"), P(EP, None, "y"), P(EP, None, "y"), P(None, EP, "y"))
    return jax.shard_map(body, mesh=fine, in_specs=in_specs, out_specs=out_specs, check_vma=False)
```

```python
import jax
import jax.numpy as jnp
from jax import lax
from jax.experimental import pallas as pl
from jax.experimental.pallas import tpu as pltpu
from jax.sharding import Mesh, PartitionSpec as P

EXPERTS = 16
MOST = 10
Z, X, C, Y = 8, 4, 2, 4
PLANE = X * C
EP = ("z", "x", "c")
XC = ("x", "c")


def exchange(value, axes):
    return lax.all_to_all(value, axes, split_axis=0, concat_axis=0, tiled=True)


def shift(value, step):
    return lax.ppermute(value, "z", [(i, (i + step) % Z) for i in range(Z)])


class Ring:
    def __init__(self, block):
        self.ahead = [block]
        self.behind = [block]
        self.far = []

    def hop(self):
        if len(self.ahead) < Z // 2:
            self.behind.append(shift(self.behind[-1], 1))
            self.ahead.append(shift(self.ahead[-1], -1))
        else:
            half = self.ahead[0].shape[0] // 2
            self.far = [shift(self.behind[-1][:half], 1), shift(self.ahead[-1][half:], -1)]
        return self

    def hold(self, value):
        last = self.far or [self.behind[-1], self.ahead[-1]]
        value, held = lax.optimization_barrier((value, last))
        if self.far:
            self.far = held
        else:
            self.behind[-1], self.ahead[-1] = held
        return value

    def pick(self, index):
        blocks = self.ahead + self.far + self.behind[:0:-1]
        return pick_pieces(index.reshape(-1), blocks)


def pick_kernel(index_ref, *refs):
    blocks, out_ref, held_ref, read_sems, write_sems = refs[:-4], *refs[-4:]
    count = out_ref.shape[0]
    half = blocks[Z // 2].shape[0]

    def read(i, carry):
        distance = index_ref[i] >> 4
        place = index_ref[i] & 15

        def copy(block, piece):
            pltpu.make_async_copy(block.at[piece], held_ref.at[i], read_sems.at[i]).start()

        for k in range(Z):
            if k == Z // 2:
                pl.when((distance == k) & (place < half))(lambda: copy(blocks[Z // 2], place))
                pl.when((distance == k) & (place >= half))(
                    lambda: copy(blocks[Z // 2 + 1], place - half)
                )
            else:
                block = blocks[k if k < Z // 2 else k + 1]
                pl.when(distance == k)(lambda block=block: copy(block, place))
        return carry

    def write(i, carry):
        pltpu.make_async_copy(blocks[0].at[0], held_ref.at[i], read_sems.at[i]).wait()
        pltpu.make_async_copy(held_ref.at[i], out_ref.at[i], write_sems.at[i]).start()
        return carry

    def finish(i, carry):
        pltpu.make_async_copy(held_ref.at[i], out_ref.at[i], write_sems.at[i]).wait()
        return carry

    lax.fori_loop(0, count, read, 0)
    lax.fori_loop(0, count, write, 0)
    lax.fori_loop(0, count, finish, 0)


def pick_pieces(index, blocks):
    count = index.shape[0]
    shape = (count,) + blocks[0].shape[1:]
    return pl.pallas_call(
        pick_kernel,
        out_shape=jax.ShapeDtypeStruct(shape, blocks[0].dtype),
        in_specs=[pl.BlockSpec(memory_space=pltpu.SMEM)]
        + [pl.BlockSpec(memory_space=pl.ANY)] * len(blocks),
        out_specs=pl.BlockSpec(memory_space=pl.ANY),
        scratch_shapes=[
            pltpu.VMEM(shape, blocks[0].dtype),
            pltpu.SemaphoreType.DMA((count,)),
            pltpu.SemaphoreType.DMA((count,)),
        ],
        name="pick_pieces",
    )(index, *blocks)


def take_rows(value, index):
    return value.at[index].get(mode="promise_in_bounds")


def body(
    tokens, route_ids, route_weights, train_map, serve_place, train_gate, train_up, train_down
):
    plane = lax.axis_index("z")
    line = lax.axis_index(XC)
    quarter = lax.axis_index("y")
    slot_count = serve_place.shape[0]
    part_count = slot_count // EXPERTS
    piece_rows = train_gate.shape[1]
    width = train_gate.shape[2]
    block_rows = piece_rows // PLANE
    steps, tok_count, model_width = tokens.shape
    out_width = model_width // Y
    own_tokens = steps * tok_count
    line_tokens = own_tokens * Z
    capacity = Z * steps * MOST // 2

    slot_iota = jnp.arange(slot_count, dtype=jnp.int32)
    inverse = jnp.sum(
        jnp.where(train_map[:, None] == slot_iota[None, :], slot_iota[:, None], 0), axis=0
    )
    relative = (inverse - plane * PLANE + slot_count) % slot_count
    place_rank = jnp.sum(
        (serve_place[:, None] == serve_place[None, :])
        & (slot_iota[None, :] < slot_iota[:, None]),
        axis=1,
    )
    near_experts = lax.dynamic_slice(serve_place, (plane * PLANE,), (PLANE,))
    near_rank = lax.dynamic_slice(place_rank, (plane * PLANE,), (PLANE,))
    near_count = jnp.sum(near_experts[:, None] == serve_place[None, :], axis=1)
    wanted = near_experts[:, None] * part_count + jnp.arange(part_count, dtype=jnp.int32)[None, :]
    chosen = take_rows(relative // PLANE * 16 + relative % PLANE, wanted)
    chosen_slot = take_rows(inverse, wanted)

    def spread(piece):
        return exchange(piece.reshape(PLANE, block_rows, width), XC)

    def gather_planes(block):
        rows = lax.all_gather(block.reshape(-1, width), "z", axis=0, tiled=True)
        return rows.reshape(slot_count, block_rows, width)

    def assemble(arrived):
        return jnp.swapaxes(arrived, 0, 1).reshape(1, part_count * piece_rows, width)

    experts = jnp.arange(EXPERTS, dtype=jnp.int32)
    hot = route_ids.reshape(own_tokens, -1)[:, :, None] == experts
    named = jnp.any(hot, axis=1).astype(jnp.bfloat16)
    weight = jnp.sum(
        jnp.where(hot, route_weights.reshape(own_tokens, -1)[:, :, None], 0.0), axis=1
    )
    high = weight.astype(jnp.bfloat16)
    rest = weight - high.astype(jnp.float32)
    middle = rest.astype(jnp.bfloat16)
    low = (rest - middle.astype(jnp.float32)).astype(jnp.bfloat16)
    own_rows = lax.dynamic_slice(
        tokens.reshape(own_tokens, model_width),
        (0, quarter * out_width),
        (own_tokens, out_width),
    )
    own_block = jnp.concatenate([own_rows, named, high, middle, low], axis=1)
    block_gate = spread(train_gate)
    block_gate, train_up, own_block = lax.optimization_barrier((block_gate, train_up, own_block))
    gate_all = gather_planes(block_gate)
    block_up = spread(train_up)
    block_up, train_down = lax.optimization_barrier((block_up, train_down))
    up_all = gather_planes(block_up)
    own_block = jnp.pad(own_block, ((0, 0), (0, -own_block.shape[1] % 128)))
    token_ring = Ring(own_block.reshape(2, own_tokens // 2, -1)).hop().hop().hop().hop()
    train_down = token_ring.hold(train_down)
    block_down = spread(train_down)
    planes = jnp.arange(Z, dtype=jnp.int32)
    line_block = token_ring.pick(((planes - plane + Z) % Z * 16)[:, None] + jnp.arange(2)[None, :])
    line_block = line_block.reshape(line_tokens, -1)
    line_rows = line_block[:, :out_width]
    line_routes = line_block[:, out_width : out_width + 4 * EXPERTS]
    token_iota = jnp.arange(line_tokens, dtype=jnp.int32)
    earlier = (token_iota[None, :] < token_iota[:, None]).astype(jnp.bfloat16)
    near_hot = near_experts[:, None] == experts[None, :]

    def place(routes, line_index):
        names = routes[..., :EXPERTS]
        seen = jnp.einsum("ut,lte->lue", earlier, names, preferred_element_type=jnp.float32)

        def of_near(table):
            return jnp.sum(
                jnp.where(near_hot[None, :, None, :], table.astype(jnp.float32)[:, None], 0.0), axis=3
            )

        near_seen = of_near(seen).astype(jnp.int32)
        turn = (near_seen + line_index[:, None, None]) % near_count[None, :, None]
        position = near_seen // near_count[None, :, None]
        sent = (of_near(names) > 0.5) & (turn == near_rank[None, :, None])
        rows = jnp.arange(capacity, dtype=jnp.int32)[None, None, :, None]
        return sent[:, :, None, :] & (position[:, :, None, :] == rows)

    own_placing = place(line_routes[None], line[None])[0].astype(jnp.bfloat16)
    send_rows = jnp.einsum(
        "spt,td->spd", own_placing, line_rows, preferred_element_type=jnp.float32
    ).astype(jnp.bfloat16)
    route_rows = line_routes.reshape(-1, out_width)
    send_rows = jnp.concatenate(
        [send_rows, jnp.broadcast_to(route_rows, (PLANE,) + route_rows.shape)], axis=1
    )
    received = exchange(send_rows, XC)
    quarters = received[:, :capacity].reshape(PLANE * capacity, out_width)
    half = quarters.shape[0] // 2
    to_next = [(i, (i + 1) % Y) for i in range(Y)]
    to_last = [(i, (i - 1) % Y) for i in range(Y)]
    from_last = lax.ppermute(quarters, "y", to_next)
    from_next = lax.ppermute(quarters, "y", to_last)
    gate_all, from_last, from_next = lax.optimization_barrier((gate_all, from_last, from_next))
    far = [
        lax.ppermute(from_last[:half], "y", to_next),
        lax.ppermute(from_next[half:], "y", to_last),
    ]
    far, block_down = lax.optimization_barrier((far, block_down))
    inputs = take_rows(
        jnp.stack([quarters, from_next, jnp.concatenate(far, axis=0), from_last]),
        (jnp.arange(Y, dtype=jnp.int32) - quarter + Y) % Y,
    )
    up_all, inputs = lax.optimization_barrier((up_all, inputs))
    routes = received[:, capacity:].reshape(PLANE, line_tokens, -1)
    placing = place(routes, jnp.arange(PLANE, dtype=jnp.int32))
    weights = sum(
        routes[..., k * EXPERTS : (k + 1) * EXPERTS].astype(jnp.float32) for k in (1, 2, 3)
    )
    own_expert = lax.dynamic_slice(near_experts, (line,), (1,))
    own_weight = jnp.sum(jnp.where(experts == own_expert, weights, 0.0), axis=2)
    own_sent = lax.dynamic_slice(
        placing, (0, line, 0, 0), (PLANE, 1, capacity, line_tokens)
    )[:, 0]
    row_weight = jnp.sum(jnp.where(own_sent, own_weight[:, None, :], 0.0), axis=2)
    placing = placing.astype(jnp.bfloat16)

    by_part = (part_count, piece_rows, width)
    serve_gate = assemble(exchange(take_rows(gate_all, chosen_slot), XC))
    arrived_up = exchange(take_rows(up_all, chosen_slot), XC)
    down_ring = Ring(block_down).hop()
    inputs = down_ring.hold(inputs)
    gate_act = jnp.einsum(
        "ymd,ydf->mf", inputs, serve_gate.reshape(by_part), preferred_element_type=jnp.float32
    )
    arrived_up, gate_act = lax.optimization_barrier((arrived_up, gate_act))
    down_ring.hop()
    serve_up = assemble(arrived_up)
    up_act = jnp.einsum(
        "ymd,ydf->mf", inputs, serve_up.reshape(by_part), preferred_element_type=jnp.float32
    )
    hidden = (jax.nn.silu(gate_act) * up_act * row_weight.reshape(-1, 1)).astype(jnp.bfloat16)
    hidden = down_ring.hold(hidden)
    down_ring.hop()

    down_ring.hop()

    plane_hidden = lax.all_gather(hidden, XC, axis=0, tiled=False).reshape(
        PLANE, PLANE, capacity, width
    )
    down_rows = down_ring.pick(chosen).reshape(PLANE, part_count, block_rows, width)
    serve_down = assemble(exchange(down_rows, XC))
    partial_value = jnp.einsum(
        "slpf,syrf->slpyr", plane_hidden, down_rows, preferred_element_type=jnp.float32
    ).astype(jnp.bfloat16)
    plane_out = jnp.einsum(
        "lspt,slpyr->yltr", placing, partial_value, preferred_element_type=jnp.float32
    ).astype(jnp.bfloat16)
    line_out = lax.psum_scatter(
        plane_out.reshape(-1, block_rows), "y", scatter_dimension=0, tiled=True
    )
    home = exchange(
        jnp.swapaxes(line_out.reshape(PLANE, Z, own_tokens, block_rows), 0, 1).reshape(
            Z * PLANE, own_tokens, block_rows
        ),
        EP,
    )
    total = jnp.sum(
        home.reshape(Z, PLANE, own_tokens, block_rows).astype(jnp.float32), axis=0
    ).astype(jnp.bfloat16)
    moe_out = jnp.swapaxes(total, 0, 1).reshape(steps, tok_count, out_width)
    return (serve_gate, serve_up, serve_down, moe_out)


def solution(mesh):
    fine = Mesh(mesh.devices.reshape(Z, X, C, Y), ("z", "x", "c", "y"))
    in_specs = (
        P(None, EP, None),
        P(None, EP, None),
        P(None, EP, None),
        P(),
        P(),
        P(EP, None, "y"),
        P(EP, None, "y"),
        P(EP, None, "y"),
    )
    out_specs = (P(EP, None, "y"), P(EP, None, "y"), P(EP, None, "y"), P(None, EP, "y"))
    return jax.shard_map(body, mesh=fine, in_specs=in_specs, out_specs=out_specs, check_vma=False)
```
